512 devices in a mesh: tile: 128 (over x, z, y_lo), layer: 4 (over y_hi, core).
Axes of the slice: x: 4, y: 4 (y_hi: 2, y_lo: 2; y = y_hi * 2 + y_lo), z: 16, core: 2. Of those that a mesh axis runs over, the one named last changes fastest.
Arguments:
- probes: float32 [8, 3, 8, 1024, 128], P(None, None, 'layer', 'tile'), may hold values from -46 to 46
- material: int32 [8, 1024, 128], P('layer', 'tile'), may hold values from 0 to 2
- lame_pairs: float32 [3, 2], replicated, may hold values from 0.5 to 5
Outputs:
- solution: float32 [8, 3, 8, 1024, 128], P(None, None, 'layer', 'tile')
- residual: float32 [8, 3, 8, 1024, 128], P(None, None, 'layer', 'tile')
The draws below stay inside these ranges and needn't reach their ends.
Inputs may be any that keep to these rules, and one draw needn't show every extreme that they name: `material`: 0 die silicon, 1 copper, 2 underfill.
All inputs are finite; a program needn't handle non-finite values.
Results may differ from the reference program's by a relative error of at most 0.0003.
Values sent between devices are 32-bit elements; how exact they have to be, the bound alone decides.
No kernel may reach another device: no remote copies, remote signals or barrier semaphores. Data moves between devices by JAX's collectives and lax.ppermute only.
A program may use at most 64 MiB of HBM per device.

```python
import math
import jax
import jax.numpy as jnp
import numpy as np
from jax import lax

NY = 128
PROBES = 8
NMAT = 3
ITERS = 2
NZ = 8
NX = 1024


def draw_probes(key, part):
    subkeys = jax.random.split(key, 3)
    full_shape = (PROBES, 3, NZ, NX, NY)
    probe_scale = jnp.exp(jax.random.uniform(subkeys[0], (PROBES, 1, 1, 1, 1), jnp.float32, math.log(0.3), math.log(3.0)))
    plane_scale = jnp.exp(jax.random.uniform(subkeys[1], (1, 1, 1, NX, 1), jnp.float32, math.log(0.3), math.log(3.0)))
    values_raw = jnp.clip(jax.random.normal(subkeys[2], full_shape, jnp.float32), -4.0, 4.0)
    return (values_raw * probe_scale * plane_scale).astype(jnp.float32)


def plant(values, stream_key, smallest, largest):
    longest = values.shape.index(max(values.shape))
    spots = []
    for shift in (0, 1):
        where = [jax.random.randint(jax.random.fold_in(stream_key, axis), (), 0, length) for axis, length in enumerate(values.shape)]
        where[longest] = (where[longest] + shift) % values.shape[longest]
        spots.append(tuple(where))
    return values.at[spots[0]].set(smallest).at[spots[1]].set(largest)


def setup_inputs(seed: int = 0) -> dict:
    keys = jax.random.split(jax.random.key(seed), 4)
    probes = draw_probes(jax.random.fold_in(keys[3], 71), 0)
    material = plant(jax.random.randint(keys[1], (NZ, NX, NY), 0, 3), jax.random.fold_in(keys[1], 1), 0, 2).astype(jnp.int32)
    lame_pairs = jnp.clip(jnp.exp(jax.random.uniform(keys[2], (NMAT, 2), jnp.float32, math.log(0.5), math.log(5.0))), 0.5, 5.0)
    return dict(probes=probes, material=material, lame_pairs=lame_pairs)


def element_tables():
    points = [0.5 - 0.5 / math.sqrt(3.0), 0.5 + 0.5 / math.sqrt(3.0)]
    offsets = np.array([[corner >> 2 & 1, corner >> 1 & 1, corner & 1] for corner in range(8)]) * 1.0
    identity = np.eye(3)
    lam_table = np.zeros((24, 24))
    mu_table = np.zeros((24, 24))
    for point_one in points:
        for point_two in points:
            for point_three in points:
                location = np.array([point_one, point_two, point_three])
                factors = np.where(offsets > 0.5, location, 1.0 - location)
                slopes = np.where(offsets > 0.5, 1.0, -1.0)
                gradients = np.zeros((8, 3))
                for coordinate in range(3):
                    others = factors.copy()
                    others[:, coordinate] = slopes[:, coordinate]
                    gradients[:, coordinate] = np.prod(others, axis=1)
                outer = gradients[:, :, None, None] * gradients[None, None, :, :]
                lam_table += 0.125 * outer.reshape(24, 24)
                gradient_dots = gradients @ gradients.T
                first_term = gradient_dots[:, None, :, None] * identity[None, :, None, :]
                second_term = gradients[:, None, None, :] * gradients.T[None, :, :, None]
                mu_table += 0.125 * (first_term + second_term).reshape(24, 24)
    return np.concatenate([lam_table, mu_table], 1).astype(np.float32)

def material_fields(material, lame_pairs):
    lam_cells = jnp.zeros(material.shape, jnp.float32)
    mu_cells = jnp.zeros(material.shape, jnp.float32)
    for kind_index in range(lame_pairs.shape[0]):
        chosen = material == kind_index
        lam_cells = lam_cells + jnp.where(chosen, lame_pairs[kind_index, 0], 0.0)
        mu_cells = mu_cells + jnp.where(chosen, lame_pairs[kind_index, 1], 0.0)
    return (lam_cells, mu_cells)

def element_forces(single, lam_cells, mu_cells, tables):
    depth_cells, width_cells, span_cells = lam_cells.shape
    cell_count = depth_cells * width_cells * span_cells
    pieces = []
    for corner in range(8):
        up_depth = corner >> 2 & 1
        up_width = corner >> 1 & 1
        up_span = corner & 1
        sliced = single[:, up_depth:up_depth + depth_cells, up_width:up_width + width_cells, :]
        if up_span:
            sliced = jnp.concatenate([sliced[..., 1:], jnp.zeros_like(sliced[..., :1])], -1)
        pieces.append(sliced.reshape(3, cell_count))
    stacked = jnp.concatenate(pieces, 0)
    scaled = jnp.concatenate([stacked * lam_cells.reshape(1, cell_count), stacked * mu_cells.reshape(1, cell_count)], 0)
    forces = jnp.dot(tables.astype(jnp.float32), scaled.astype(jnp.float32), precision=lax.Precision.HIGHEST, preferred_element_type=jnp.float32)
    forces = forces.reshape(8, 3, depth_cells, width_cells, span_cells)
    summed = jnp.zeros((3, depth_cells + 1, width_cells + 1, span_cells), jnp.float32)
    for corner in range(8):
        up_depth = corner >> 2 & 1
        up_width = corner >> 1 & 1
        up_span = corner & 1
        contrib = forces[corner]
        if up_span:
            contrib = jnp.concatenate([jnp.zeros_like(contrib[..., :1]), contrib[..., :-1]], -1)
        summed = summed + jnp.pad(contrib, ((0, 0), (up_depth, 1 - up_depth), (up_width, 1 - up_width), (0, 0)))
    return summed

def stiffness_apply(nodal_values, lam_cells, mu_cells, tables):
    extended = jnp.pad(nodal_values, ((0, 0), (0, 0), (0, 1), (0, 1), (0, 0)))
    result = lax.map(lambda single: element_forces(single, lam_cells, mu_cells, tables), extended)
    return result[:, :, :-1, :-1, :]

def gram(left_block, right_block):
    count_rows = left_block.shape[0]
    return jnp.dot(left_block.reshape(count_rows, -1).astype(jnp.float32), right_block.reshape(count_rows, -1).T.astype(jnp.float32), precision=lax.Precision.HIGHEST, preferred_element_type=jnp.float32)

def combine(coefficients, block_rows):
    count_rows = block_rows.shape[0]
    mixed = jnp.dot(coefficients.T.astype(jnp.float32), block_rows.reshape(count_rows, -1).astype(jnp.float32), precision=lax.Precision.HIGHEST, preferred_element_type=jnp.float32)
    return mixed.reshape(block_rows.shape)

def spd_solve(matrix, right_side):
    lower_factor = jnp.linalg.cholesky(matrix)
    middle = lax.linalg.triangular_solve(lower_factor, right_side, left_side=True, lower=True)
    return lax.linalg.triangular_solve(lower_factor, middle, left_side=True, lower=True, transpose_a=True)

def symmetric(matrix):
    return 0.5 * (matrix + matrix.T)

def reference(probes, material, lame_pairs):
    lam_cells, mu_cells = material_fields(material, lame_pairs)
    tables = jnp.asarray(element_tables(), jnp.float32)
    solution = jnp.zeros_like(probes)
    residual = probes
    direction = probes
    norms_now = symmetric(gram(residual, residual))
    for turn_index in range(ITERS):
        image_block = stiffness_apply(direction, lam_cells, mu_cells, tables)
        curvature = symmetric(gram(direction, image_block))
        step_alpha = spd_solve(curvature, norms_now)
        solution = solution + combine(step_alpha, direction)
        residual = residual - combine(step_alpha, image_block)
        if turn_index + 1 < ITERS:
            norms_next = symmetric(gram(residual, residual))
            step_beta = spd_solve(norms_now, norms_next)
            direction = residual + combine(step_beta, direction)
            norms_now = norms_next
    return (solution, residual)
```

```python
import jax
import jax.numpy as jnp
from jax import lax
from jax.experimental import pallas as pl
from jax.experimental.pallas import tpu as pltpu
from jax.sharding import Mesh
from jax.sharding import PartitionSpec as P

TILE = ("tile_0", "tile_1", "tile_2")
LAYER = ("layer_0", "layer_1")
PLANE = ("tile_0", "tile_2", "layer_0", "layer_1")
COLUMN = "tile_1"

PROBES = 8
OWN_Z = 2
OWN_X = 8
WIDE_X = OWN_X + 4
WIDE_Z = OWN_Z + 4
SPAN = 128
ROWS = 3 * OWN_Z * OWN_X
EDGE = 13
FULL = 6 * WIDE_X + 6
F32 = jnp.float32
HIGHEST = lax.Precision.HIGHEST


def vregs(*shape):
    return jax.ShapeDtypeStruct((*shape, 8, SPAN), F32)


def call(kernel, out_shape, scratch=(), smem=()):
    def run(*args):
        specs = [
            pl.BlockSpec(memory_space=pltpu.SMEM if i in smem else pltpu.VMEM)
            for i in range(len(args))
        ]
        outs = out_shape if isinstance(out_shape, (list, tuple)) else None
        out_specs = (
            [pl.BlockSpec(memory_space=pltpu.VMEM)] * len(outs)
            if outs
            else pl.BlockSpec(memory_space=pltpu.VMEM)
        )
        return pl.pallas_call(
            kernel,
            out_shape=out_shape,
            in_specs=specs,
            out_specs=out_specs,
            scratch_shapes=list(scratch),
            name=kernel.__name__,
        )(*args)

    return run


def pack_kernel(lame, probes, material, own, to_y, to_z):
    odd = lax.axis_index("tile_2") == 1
    for z in range(OWN_Z):
        for x in range(OWN_X):
            for c in range(3):
                own[(z * OWN_X + x) * 3 + c] = probes[
                    pl.ds((c * OWN_Z + z) * OWN_X + x, PROBES, stride=ROWS), :
                ]
    fields = {}
    for z in range(OWN_Z):
        kinds = material[z]
        for k in range(2):
            value = jnp.where(
                kinds == 0, lame[0, k], jnp.where(kinds == 1, lame[1, k], lame[2, k])
            )
            fields[k, z] = value * (1.0 / 16.0)
            own[48 + k * 2 + z] = fields[k, z]
    first_y = jnp.where(odd, 0, OWN_X - 2)
    first_z = jnp.where(odd, OWN_X - 2, 0)
    for first, to in ((first_y, to_y), (first_z, to_z)):
        for z in range(OWN_Z):
            for xx in range(2):
                for c in range(3):
                    to[(z * 2 + xx) * 3 + c] = own[(z * OWN_X + first + xx) * 3 + c]
    low = jnp.concatenate([fields[k, z][0:2] for k in range(2) for z in range(2)], 0)
    high = jnp.concatenate([fields[k, z][6:8] for k in range(2) for z in range(2)], 0)
    to_y[12] = jnp.where(odd, low, high)
    to_z[12] = jnp.where(odd, high, low)


def widen_kernel(own, from_y, from_z, full):
    odd = lax.axis_index("tile_2") == 1
    for z in range(OWN_Z):
        for c in range(3):
            for x in range(OWN_X):
                full[(z * WIDE_X + 2 + x) * 3 + c] = own[(z * OWN_X + x) * 3 + c]
            for xx in range(2):
                at = (z * 2 + xx) * 3 + c
                full[(z * WIDE_X + xx) * 3 + c] = jnp.where(odd, from_y[at], from_z[at])
                full[(z * WIDE_X + 10 + xx) * 3 + c] = jnp.where(odd, from_z[at], from_y[at])
    for i in range(4):
        full[72 + i] = own[48 + i]
    full[76] = jnp.where(odd, from_y[12], from_z[12])
    full[77] = jnp.where(odd, from_z[12], from_y[12])


def stress(modes, lam, mu):
    a, b, e, p, q, r, t = modes
    third = 1.0 / 3.0
    lam3 = lam * third
    mu3 = mu * third
    both = mu + lam3
    top = (4.0 * mu + lam) * (1.0 / 9.0)
    twice = mu + mu
    trace = lam * (a[0] + b[1] + e[2])
    s01 = mu * (b[0] + a[1])
    s02 = mu * (e[0] + a[2])
    s12 = mu * (e[1] + b[2])
    aa = (twice * a[0] + trace, s01, s02)
    bb = (s01, twice * b[1] + trace, s12)
    ee = (s02, s12, twice * e[2] + trace)
    mixed = p[2] + q[1] + r[0]
    pp = (both * p[0] + lam3 * r[2], both * p[1] + lam3 * q[2], mu3 * (p[2] + mixed))
    qq = (both * q[0] + lam3 * r[1], mu3 * (q[1] + mixed), both * q[2] + lam3 * p[1])
    rr = (mu3 * (r[0] + mixed), both * r[1] + lam3 * q[0], both * r[2] + lam3 * p[0])
    tt = tuple(top * t[c] for c in range(3))
    return aa, bb, ee, pp, qq, rr, tt


def element_column(load, fields, height, emit):
    def along_x(z):
        values = []
        for c in range(3):
            s0, d0, s1, d1 = load(z, c)
            values.append((s0 + s1, s1 - s0, d0 + d1, d1 - d0))
        return values

    below = along_x(0)
    carried = None
    for z in range(height):
        above = along_x(z + 1)
        modes = tuple(
            tuple(
                above[c][kind] - below[c][kind] if minus else above[c][kind] + below[c][kind]
                for c in range(3)
            )
            for kind, minus in (
                (0, True),
                (1, False),
                (2, False),
                (1, True),
                (2, True),
                (3, False),
                (3, True),
            )
        )
        lam, mu = fields(z)
        aa, bb, ee, pp, qq, rr, tt = stress(modes, lam, mu)
        if carried is not None:
            emit(
                z,
                [
                    (
                        carried[c][0] - aa[c],
                        carried[c][1] + (bb[c] - pp[c]),
                        carried[c][2] + (ee[c] - qq[c]),
                        carried[c][3] + (rr[c] - tt[c]),
                    )
                    for c in range(3)
                ],
            )
        carried = [(aa[c], bb[c] + pp[c], ee[c] + qq[c], rr[c] + tt[c]) for c in range(3)]
        below = above


def stencil_kernel(full, from_a, from_b, block, message, pair, pair_one, lams, mus, carry):
    core = lax.axis_index("layer_1")
    layer = lax.axis_index("layer_0") * 2 + core
    tile = (lax.axis_index("tile_0") * 16 + lax.axis_index("tile_1")) * 2 + lax.axis_index("tile_2")
    lanes = lax.broadcasted_iota(jnp.int32, (8, SPAN), 1)
    not_last = jnp.where(lanes == SPAN - 1, 0.0, 1.0).astype(F32)
    not_first = jnp.where(lanes == 0, 0.0, 1.0).astype(F32)
    keep_z = jnp.where(layer == 3, 0.0, 1.0).astype(F32)
    keep_x = jnp.where(tile == 127, 0.0, 1.0).astype(F32)

    def spread(value):
        after = pltpu.roll(value, SPAN - 1, 1) * not_last
        return value + after, after - value

    offset_a = jnp.where(core == 0, 4, 0)
    offset_b = jnp.where(core == 0, 0, 4)
    for source, offset in ((full, 2), (from_a, offset_a), (from_b, offset_b)):

        def fill(x, _, source=source, offset=offset):
            for z in range(OWN_Z):
                for c in range(3):
                    value = source[(z * WIDE_X + x) * 3 + c]
                    at = (((offset + z) * WIDE_X + x) * 3 + c) * 2
                    both = spread(value)
                    pair[at] = both[0]
                    pair[at + 1] = both[1]
            return 0

        lax.fori_loop(0, WIDE_X, fill, 0)
        for k, target in ((0, lams), (1, mus)):
            for z in range(OWN_Z):
                for x in range(WIDE_X):
                    if x < 2:
                        row = source[76, k * 4 + z * 2 + x : k * 4 + z * 2 + x + 1, :]
                    elif x < 10:
                        row = source[72 + k * 2 + z, x - 2 : x - 1, :]
                    else:
                        row = source[77, k * 4 + z * 2 + x - 10 : k * 4 + z * 2 + x - 9, :]
                    target[(offset + z) * WIDE_X + x] = jnp.broadcast_to(row, (8, SPAN))
    for x in range(OWN_X):
        for z in range(OWN_Z):
            for c in range(3):
                at = ((x + 2) * 6 + z * 3 + c) * SPAN
                block[0:8, at : at + SPAN] = full[(z * WIDE_X + 2 + x) * 3 + c]

    def finish(x, z, c, slot, parts):
        ss, ds, sd, dd = parts
        total_s = carry[slot] + (ss - ds)
        total_d = carry[slot + 1] + (sd - dd)
        carry[slot] = ss + ds
        carry[slot + 1] = sd + dd
        return (total_s - total_d) + pltpu.roll(total_s + total_d, 1, 1) * not_first

    carry[...] = jnp.zeros(carry.shape, F32)

    def first(x, _):
        def load(z, c):
            at = ((z * WIDE_X + x) * 3 + c) * 2
            return pair[at], pair[at + 1], pair[at + 6], pair[at + 7]

        def fields(z):
            return lams[z * WIDE_X + x], mus[z * WIDE_X + x]

        inside = jnp.where(x == 10, keep_x, 1.0)

        def emit(z, forces):
            keep = inside * keep_z if z == 4 else inside
            for c in range(3):
                value = finish(x, z, c, ((z - 1) * 3 + c) * 2, forces[c]) * keep
                if z in (2, 3):
                    at = pl.multiple_of((x * 6 + (z - 2) * 3 + c) * SPAN, SPAN)
                    block[8:16, pl.ds(at, SPAN)] = value
                both = spread(value)
                at = (((z - 1) * WIDE_X + x) * 3 + c) * 2
                pair_one[at] = both[0]
                pair_one[at + 1] = both[1]

        element_column(load, fields, 5, emit)
        return 0

    lax.fori_loop(0, WIDE_X - 1, first, 0)
    carry[...] = jnp.zeros(carry.shape, F32)

    def second(x, _):
        def load(z, c):
            at = ((z * WIDE_X + x) * 3 + c) * 2
            return pair_one[at], pair_one[at + 1], pair_one[at + 6], pair_one[at + 7]

        def fields(z):
            return lams[(z + 1) * WIDE_X + x], mus[(z + 1) * WIDE_X + x]

        def emit(z, forces):
            for c in range(3):
                value = finish(x, z, c, ((z - 1) * 3 + c) * 2, forces[c])
                at = pl.multiple_of((x * 6 + (z - 1) * 3 + c) * SPAN, SPAN)
                block[16:24, pl.ds(at, SPAN)] = value

        element_column(load, fields, 3, emit)
        return 0

    lax.fori_loop(1, WIDE_X - 2, second, 0)
    every = block[:, 12 * SPAN : 60 * SPAN]
    grams = lax.dot_general(
        every[0:16], every, (((1,), (1,)), ((), ())), precision=HIGHEST, preferred_element_type=F32
    )
    wide = jnp.concatenate([grams, jnp.zeros((16, SPAN - 24), F32)], 1)
    packed = jnp.where(lanes < 16, wide[0:8], pltpu.roll(wide[8:16], 8, 1))
    for i in range(message.shape[0]):
        message[i] = packed


def total_kernel(parts, message):
    total = parts[0]
    for i in range(1, parts.shape[0]):
        total = total + parts[i]
    for i in range(message.shape[0]):
        message[i] = total


def eliminate(table, first):
    rows = lax.broadcasted_iota(jnp.int32, (8, SPAN), 0)
    for k in range(8):
        pivot_row = jnp.broadcast_to(table[k : k + 1, :], (8, SPAN))
        column = jnp.broadcast_to(table[:, first + k : first + k + 1], (8, SPAN))
        pivot = jnp.broadcast_to(table[k : k + 1, first + k : first + k + 1], (8, SPAN))
        scaled = pivot_row / pivot
        table = jnp.where(rows == k, scaled, table - column * scaled)
    return table


def times(left, first, right):
    total = None
    for k in range(8):
        column = jnp.broadcast_to(left[:, first + k : first + k + 1], (8, SPAN))
        row = jnp.broadcast_to(right[k : k + 1, :], (8, SPAN))
        total = column * row if total is None else total + column * row
    return total


def final_kernel(parts, block, solution_rows, residual_rows):
    table = parts[0]
    for i in range(1, parts.shape[0]):
        table = table + parts[i]
    lanes = lax.broadcasted_iota(jnp.int32, (8, SPAN), 1)
    solved = eliminate(table, 8)
    product = times(table, 16, solved)
    shifted = pltpu.roll(table, SPAN - 8, 1)
    second = jnp.where(lanes < 8, product - shifted, shifted - product)
    coef_c = jnp.where(lanes < 8, eliminate(second, 16), 0.0)
    coef_b = jnp.where(lanes < 8, solved + times(solved, 16, coef_c), 0.0)
    coefs = jnp.concatenate(
        [coef_b, -coef_c - pltpu.roll(coef_b, 8, 1), pltpu.roll(coef_c, 8, 1)], 0
    )[:, 0:16]
    every = block[:, 12 * SPAN : 60 * SPAN]
    mixed = lax.dot_general(
        coefs, every, (((0,), (0,)), ((), ())), precision=HIGHEST, preferred_element_type=F32
    )
    for x in range(OWN_X):
        for z in range(OWN_Z):
            for c in range(3):
                at = (x * 6 + z * 3 + c) * SPAN
                row = (c * OWN_Z + z) * OWN_X + x
                solution_rows[pl.ds(row, PROBES, stride=ROWS), :] = mixed[0:8, at : at + SPAN]
                residual_rows[pl.ds(row, PROBES, stride=ROWS), :] = (
                    every[0:8, at : at + SPAN] + mixed[8:16, at : at + SPAN]
                )


def body(probes, material, lame_pairs):
    tiles = lax.axis_size(TILE)
    in_y = [(i, i ^ 1) for i in range(tiles)]
    in_z = [(i, ((i + 1) ^ 1) - 1) for i in range(1, tiles - 1)]
    in_core = [(0, 1), (1, 0), (2, 3), (3, 2)]
    in_chip = [(1, 2), (2, 1)]
    own, to_y, to_z = call(pack_kernel, (vregs(52), vregs(EDGE), vregs(EDGE)), smem=(0,))(
        lame_pairs, probes.reshape(PROBES * ROWS, SPAN), material
    )
    from_z = lax.ppermute(to_z, TILE, in_z)
    from_y = lax.ppermute(to_y, TILE, in_y)
    full = call(widen_kernel, vregs(FULL))(own, from_y, from_z)
    from_b = lax.ppermute(full, LAYER, in_chip)
    from_a = lax.ppermute(full, LAYER, in_core)
    planes = lax.axis_size(PLANE)
    columns = lax.axis_size(COLUMN)
    block, message = call(
        stencil_kernel,
        (jax.ShapeDtypeStruct((24, 6 * WIDE_X * SPAN), F32), vregs(planes)),
        scratch=(
            pltpu.VMEM((WIDE_Z * WIDE_X * 6, 8, SPAN), F32),
            pltpu.VMEM(((OWN_Z + 2) * WIDE_X * 6, 8, SPAN), F32),
            pltpu.VMEM((WIDE_Z * WIDE_X, 8, SPAN), F32),
            pltpu.VMEM((WIDE_Z * WIDE_X, 8, SPAN), F32),
            pltpu.VMEM((24, 8, SPAN), F32),
        ),
    )(full, from_a, from_b)
    parts = lax.all_to_all(message, PLANE, 0, 0, tiled=True)
    message = call(total_kernel, vregs(columns))(parts)
    parts = lax.all_to_all(message, COLUMN, 0, 0, tiled=True)
    rows = jax.ShapeDtypeStruct((PROBES * ROWS, SPAN), F32)
    solution_rows, residual_rows = call(final_kernel, (rows, rows))(parts, block)
    return solution_rows.reshape(probes.shape), residual_rows.reshape(probes.shape)


def solution(mesh):
    split = Mesh(
        mesh.devices.reshape(4, 16, 2, 2, 2), ("tile_0", "tile_1", "tile_2", "layer_0", "layer_1")
    )
    spread = P(None, None, LAYER, TILE, None)
    return jax.shard_map(
        body,
        mesh=split,
        in_specs=(spread, P(LAYER, TILE, None), P()),
        out_specs=(spread, spread),
        check_vma=False,
    )
```

```python
import jax
import jax.numpy as jnp
from jax import lax
from jax.experimental import pallas as pl
from jax.experimental.pallas import tpu as pltpu
from jax.sharding import Mesh
from jax.sharding import PartitionSpec as P

TILE = ("tile_0", "tile_1", "tile_2")
LAYER = ("layer_0", "layer_1")
PLANE = ("tile_0", "tile_2", "layer_0", "layer_1")
COLUMN = "tile_1"

PROBES = 8
OWN_Z = 2
OWN_X = 8
WIDE_X = OWN_X + 4
WIDE_Z = OWN_Z + 4
SPAN = 128
ROWS = 3 * OWN_Z * OWN_X
EDGE = 13
FULL = 6 * WIDE_X + 6
F32 = jnp.float32
HIGHEST = lax.Precision.HIGHEST


def vregs(*shape):
    return pltpu.VMEM((*shape, 8, SPAN), F32)


def call(kernel, out_shape, scratch=(), smem=(), outside=()):
    def run(*args):
        specs = [
            pl.BlockSpec(memory_space=pltpu.SMEM if i in smem else pltpu.VMEM)
            for i in range(len(args))
        ]
        args = [
            arg
            if i in smem or i in outside
            else pltpu.with_memory_space_constraint(arg, pltpu.VMEM)
            for i, arg in enumerate(args)
        ]
        outs = out_shape if isinstance(out_shape, (list, tuple)) else None
        out_specs = (
            [pl.BlockSpec(memory_space=pltpu.VMEM)] * len(outs)
            if outs
            else pl.BlockSpec(memory_space=pltpu.VMEM)
        )
        return pl.pallas_call(
            kernel,
            out_shape=out_shape,
            in_specs=specs,
            out_specs=out_specs,
            scratch_shapes=list(scratch),
            name=kernel.__name__,
        )(*args)

    return run


def pack_kernel(lame, probes, material, own, to_y, to_z):
    odd = lax.axis_index("tile_2") == 1
    for z in range(OWN_Z):
        for x in range(OWN_X):
            for c in range(3):
                own[(z * OWN_X + x) * 3 + c] = probes[
                    pl.ds((c * OWN_Z + z) * OWN_X + x, PROBES, stride=ROWS), :
                ]
    fields = {}
    for z in range(OWN_Z):
        kinds = material[z]
        for k in range(2):
            value = jnp.where(
                kinds == 0, lame[k, 0], jnp.where(kinds == 1, lame[k, 1], lame[k, 2])
            )
            fields[k, z] = value * (1.0 / 16.0)
            own[48 + k * 2 + z] = fields[k, z]
    first_y = jnp.where(odd, 0, OWN_X - 2)
    first_z = jnp.where(odd, OWN_X - 2, 0)
    for first, to in ((first_y, to_y), (first_z, to_z)):
        for z in range(OWN_Z):
            for xx in range(2):
                for c in range(3):
                    to[(z * 2 + xx) * 3 + c] = own[(z * OWN_X + first + xx) * 3 + c]
    low = jnp.concatenate([fields[k, z][0:2] for k in range(2) for z in range(2)], 0)
    high = jnp.concatenate([fields[k, z][6:8] for k in range(2) for z in range(2)], 0)
    to_y[12] = jnp.where(odd, low, high)
    to_z[12] = jnp.where(odd, high, low)


def widen_kernel(own, from_y, from_z, full):
    odd = lax.axis_index("tile_2") == 1
    for z in range(OWN_Z):
        for c in range(3):
            for x in range(OWN_X):
                full[(z * WIDE_X + 2 + x) * 3 + c] = own[(z * OWN_X + x) * 3 + c]
            for xx in range(2):
                at = (z * 2 + xx) * 3 + c
                full[(z * WIDE_X + xx) * 3 + c] = jnp.where(odd, from_y[at], from_z[at])
                full[(z * WIDE_X + 10 + xx) * 3 + c] = jnp.where(odd, from_z[at], from_y[at])
    for i in range(4):
        full[72 + i] = own[48 + i]
    full[76] = jnp.where(odd, from_y[12], from_z[12])
    full[77] = jnp.where(odd, from_z[12], from_y[12])


def stress(modes, lam, mu):
    a, b, e, p, q, r, t = modes
    third = 1.0 / 3.0
    lam3 = lam * third
    mu3 = mu * third
    both = mu + lam3
    top = (4.0 * mu + lam) * (1.0 / 9.0)
    twice = mu + mu
    trace = lam * (a[0] + b[1] + e[2])
    s01 = mu * (b[0] + a[1])
    s02 = mu * (e[0] + a[2])
    s12 = mu * (e[1] + b[2])
    aa = (twice * a[0] + trace, s01, s02)
    bb = (s01, twice * b[1] + trace, s12)
    ee = (s02, s12, twice * e[2] + trace)
    mixed = p[2] + q[1] + r[0]
    pp = (both * p[0] + lam3 * r[2], both * p[1] + lam3 * q[2], mu3 * (p[2] + mixed))
    qq = (both * q[0] + lam3 * r[1], mu3 * (q[1] + mixed), both * q[2] + lam3 * p[1])
    rr = (mu3 * (r[0] + mixed), both * r[1] + lam3 * q[0], both * r[2] + lam3 * p[0])
    tt = tuple(top * t[c] for c in range(3))
    return aa, bb, ee, pp, qq, rr, tt


def element_column(load, fields, height, emit):
    def along_x(z):
        values = []
        for c in range(3):
            s0, d0, s1, d1 = load(z, c)
            values.append((s0 + s1, s1 - s0, d0 + d1, d1 - d0))
        return values

    below = along_x(0)
    carried = None
    for z in range(height):
        above = along_x(z + 1)
        modes = tuple(
            tuple(
                above[c][kind] - below[c][kind] if minus else above[c][kind] + below[c][kind]
                for c in range(3)
            )
            for kind, minus in (
                (0, True),
                (1, False),
                (2, False),
                (1, True),
                (2, True),
                (3, False),
                (3, True),
            )
        )
        lam, mu = fields(z)
        aa, bb, ee, pp, qq, rr, tt = stress(modes, lam, mu)
        if carried is not None:
            emit(
                z,
                [
                    (
                        carried[c][0] - aa[c],
                        carried[c][1] + (bb[c] - pp[c]),
                        carried[c][2] + (ee[c] - qq[c]),
                        carried[c][3] + (rr[c] - tt[c]),
                    )
                    for c in range(3)
                ],
            )
        carried = [(aa[c], bb[c] + pp[c], ee[c] + qq[c], rr[c] + tt[c]) for c in range(3)]
        below = above


def stencil_kernel(full, from_a, from_b, block, message, pair, pair_one, lams, mus, carry):
    core = lax.axis_index("layer_1")
    layer = lax.axis_index("layer_0") * 2 + core
    tile = (lax.axis_index("tile_0") * 16 + lax.axis_index("tile_1")) * 2 + lax.axis_index("tile_2")
    lanes = lax.broadcasted_iota(jnp.int32, (8, SPAN), 1)
    not_last = jnp.where(lanes == SPAN - 1, 0.0, 1.0).astype(F32)
    not_first = jnp.where(lanes == 0, 0.0, 1.0).astype(F32)
    keep_z = jnp.where(layer == 3, 0.0, 1.0).astype(F32)
    keep_x = jnp.where(tile == 127, 0.0, 1.0).astype(F32)

    def spread(value):
        after = pltpu.roll(value, SPAN - 1, 1) * not_last
        return value + after, after - value

    offset_a = jnp.where(core == 0, 4, 0)
    offset_b = jnp.where(core == 0, 0, 4)
    for source, offset in ((full, 2), (from_a, offset_a), (from_b, offset_b)):

        def fill(x, _, source=source, offset=offset):
            for z in range(OWN_Z):
                for c in range(3):
                    value = source[(z * WIDE_X + x) * 3 + c]
                    at = (((offset + z) * WIDE_X + x) * 3 + c) * 2
                    both = spread(value)
                    pair[at] = both[0]
                    pair[at + 1] = both[1]
            return 0

        lax.fori_loop(0, WIDE_X, fill, 0)
        for k, target in ((0, lams), (1, mus)):
            for z in range(OWN_Z):
                for x in range(WIDE_X):
                    if x < 2:
                        row = source[76, k * 4 + z * 2 + x : k * 4 + z * 2 + x + 1, :]
                    elif x < 10:
                        row = source[72 + k * 2 + z, x - 2 : x - 1, :]
                    else:
                        row = source[77, k * 4 + z * 2 + x - 10 : k * 4 + z * 2 + x - 9, :]
                    target[(offset + z) * WIDE_X + x] = jnp.broadcast_to(row, (8, SPAN))
    for x in range(OWN_X):
        for z in range(OWN_Z):
            for c in range(3):
                at = ((x + 2) * 6 + z * 3 + c) * SPAN
                block[0:8, at : at + SPAN] = full[(z * WIDE_X + 2 + x) * 3 + c]

    def finish(x, z, c, slot, parts):
        ss, ds, sd, dd = parts
        total_s = carry[slot] + (ss - ds)
        total_d = carry[slot + 1] + (sd - dd)
        carry[slot] = ss + ds
        carry[slot + 1] = sd + dd
        return (total_s - total_d) + pltpu.roll(total_s + total_d, 1, 1) * not_first

    carry[...] = jnp.zeros(carry.shape, F32)

    def first(x, _):
        def load(z, c):
            at = ((z * WIDE_X + x) * 3 + c) * 2
            return pair[at], pair[at + 1], pair[at + 6], pair[at + 7]

        def fields(z):
            return lams[z * WIDE_X + x], mus[z * WIDE_X + x]

        inside = jnp.where(x == 10, keep_x, 1.0)

        def emit(z, forces):
            keep = inside * keep_z if z == 4 else inside
            for c in range(3):
                value = finish(x, z, c, ((z - 1) * 3 + c) * 2, forces[c]) * keep
                if z in (2, 3):
                    at = pl.multiple_of((x * 6 + (z - 2) * 3 + c) * SPAN, SPAN)
                    block[8:16, pl.ds(at, SPAN)] = value
                both = spread(value)
                at = (((z - 1) * WIDE_X + x) * 3 + c) * 2
                pair_one[at] = both[0]
                pair_one[at + 1] = both[1]

        element_column(load, fields, 5, emit)
        return 0

    lax.fori_loop(0, WIDE_X - 1, first, 0)
    carry[...] = jnp.zeros(carry.shape, F32)

    def second(x, _):
        def load(z, c):
            at = ((z * WIDE_X + x) * 3 + c) * 2
            return pair_one[at], pair_one[at + 1], pair_one[at + 6], pair_one[at + 7]

        def fields(z):
            return lams[(z + 1) * WIDE_X + x], mus[(z + 1) * WIDE_X + x]

        def emit(z, forces):
            for c in range(3):
                value = finish(x, z, c, ((z - 1) * 3 + c) * 2, forces[c])
                at = pl.multiple_of((x * 6 + (z - 1) * 3 + c) * SPAN, SPAN)
                block[16:24, pl.ds(at, SPAN)] = value

        element_column(load, fields, 3, emit)
        return 0

    lax.fori_loop(1, WIDE_X - 2, second, 0)
    every = block[:, 12 * SPAN : 60 * SPAN]
    grams = lax.dot_general(
        every[0:16], every, (((1,), (1,)), ((), ())), precision=HIGHEST, preferred_element_type=F32
    )
    wide = jnp.concatenate([grams, jnp.zeros((16, SPAN - 24), F32)], 1)
    packed = jnp.where(lanes < 16, wide[0:8], pltpu.roll(wide[8:16], 8, 1))
    for i in range(message.shape[0]):
        message[i] = packed


def total_kernel(parts, message):
    total = parts[0]
    for i in range(1, parts.shape[0]):
        total = total + parts[i]
    for i in range(message.shape[0]):
        message[i] = total


def eliminate(table, first):
    rows = lax.broadcasted_iota(jnp.int32, (8, SPAN), 0)
    for k in range(8):
        pivot_row = jnp.broadcast_to(table[k : k + 1, :], (8, SPAN))
        column = jnp.broadcast_to(table[:, first + k : first + k + 1], (8, SPAN))
        pivot = jnp.broadcast_to(table[k : k + 1, first + k : first + k + 1], (8, SPAN))
        scaled = pivot_row / pivot
        table = jnp.where(rows == k, scaled, table - column * scaled)
    return table


def times(left, first, right):
    total = None
    for k in range(8):
        column = jnp.broadcast_to(left[:, first + k : first + k + 1], (8, SPAN))
        row = jnp.broadcast_to(right[k : k + 1, :], (8, SPAN))
        total = column * row if total is None else total + column * row
    return total


def final_kernel(parts, block, solution_rows, residual_rows):
    table = parts[0]
    for i in range(1, parts.shape[0]):
        table = table + parts[i]
    lanes = lax.broadcasted_iota(jnp.int32, (8, SPAN), 1)
    solved = eliminate(table, 8)
    product = times(table, 16, solved)
    shifted = pltpu.roll(table, SPAN - 8, 1)
    second = jnp.where(lanes < 8, product - shifted, shifted - product)
    coef_c = jnp.where(lanes < 8, eliminate(second, 16), 0.0)
    coef_b = jnp.where(lanes < 8, solved + times(solved, 16, coef_c), 0.0)
    coefs = jnp.concatenate(
        [coef_b, -coef_c - pltpu.roll(coef_b, 8, 1), pltpu.roll(coef_c, 8, 1)], 0
    )[:, 0:16]
    every = block[:, 12 * SPAN : 60 * SPAN]
    mixed = lax.dot_general(
        coefs, every, (((0,), (0,)), ((), ())), precision=HIGHEST, preferred_element_type=F32
    )
    for x in range(OWN_X):
        for z in range(OWN_Z):
            for c in range(3):
                at = (x * 6 + z * 3 + c) * SPAN
                row = (c * OWN_Z + z) * OWN_X + x
                solution_rows[pl.ds(row, PROBES, stride=ROWS), :] = mixed[0:8, at : at + SPAN]
                residual_rows[pl.ds(row, PROBES, stride=ROWS), :] = (
                    every[0:8, at : at + SPAN] + mixed[8:16, at : at + SPAN]
                )


def body(probes, material, lame_pairs):
    tiles = lax.axis_size(TILE)
    in_y = [(i, i ^ 1) for i in range(tiles)]
    in_z = [(i, ((i + 1) ^ 1) - 1) for i in range(1, tiles - 1)]
    in_core = [(0, 1), (1, 0), (2, 3), (3, 2)]
    in_chip = [(1, 2), (2, 1)]
    own, to_y, to_z = call(pack_kernel, (vregs(52), vregs(EDGE), vregs(EDGE)), smem=(0,), outside=(1, 2))(
        lame_pairs.T, probes.reshape(PROBES * ROWS, SPAN), material
    )
    from_z = lax.ppermute(to_z, TILE, in_z)
    from_y = lax.ppermute(to_y, TILE, in_y)
    full = call(widen_kernel, vregs(FULL))(own, from_y, from_z)
    from_b = lax.ppermute(full, LAYER, in_chip)
    from_a = lax.ppermute(full, LAYER, in_core)
    planes = lax.axis_size(PLANE)
    columns = lax.axis_size(COLUMN)
    block, message = call(
        stencil_kernel,
        (pltpu.VMEM((24, 6 * WIDE_X * SPAN), F32), vregs(planes)),
        scratch=(
            pltpu.VMEM((WIDE_Z * WIDE_X * 6, 8, SPAN), F32),
            pltpu.VMEM(((OWN_Z + 2) * WIDE_X * 6, 8, SPAN), F32),
            pltpu.VMEM((WIDE_Z * WIDE_X, 8, SPAN), F32),
            pltpu.VMEM((WIDE_Z * WIDE_X, 8, SPAN), F32),
            pltpu.VMEM((24, 8, SPAN), F32),
        ),
    )(full, from_a, from_b)
    parts = lax.all_to_all(message, PLANE, 0, 0, tiled=True)
    message = call(total_kernel, vregs(columns))(parts)
    parts = lax.all_to_all(message, COLUMN, 0, 0, tiled=True)
    rows = jax.ShapeDtypeStruct((PROBES * ROWS, SPAN), F32)
    solution_rows, residual_rows = call(final_kernel, (rows, rows))(parts, block)
    return solution_rows.reshape(probes.shape), residual_rows.reshape(probes.shape)


def solution(mesh):
    split = Mesh(
        mesh.devices.reshape(4, 16, 2, 2, 2), ("tile_0", "tile_1", "tile_2", "layer_0", "layer_1")
    )
    spread = P(None, None, LAYER, TILE, None)
    return jax.shard_map(
        body,
        mesh=split,
        in_specs=(spread, P(LAYER, TILE, None), P()),
        out_specs=(spread, spread),
        check_vma=False,
    )
```

```python
import jax
import jax.numpy as jnp
from jax import lax
from jax.experimental import pallas as pl
from jax.experimental.pallas import tpu as pltpu
from jax.sharding import Mesh
from jax.sharding import PartitionSpec as P

TILE = ("tile_0", "tile_1", "tile_2")
LAYER = ("layer_0", "layer_1")
PLANE = ("tile_0", "tile_2", "layer_0", "layer_1")
COLUMN = "tile_1"

PROBES = 8
OWN_Z = 2
OWN_X = 8
WIDE_X = OWN_X + 4
SPAN = 128
ROWS = 3 * OWN_Z * OWN_X
EDGE = 13
FULL = 70
SIDE = 6 * WIDE_X
HALF = 3 * OWN_X
F32 = jnp.float32
HIGHEST = lax.Precision.HIGHEST


def vregs(*shape):
    return pltpu.VMEM((*shape, 8, SPAN), F32)


def call(kernel, out_shape, scratch=(), smem=(), outside=()):
    def run(*args):
        specs = [
            pl.BlockSpec(memory_space=pltpu.SMEM if i in smem else pltpu.VMEM)
            for i in range(len(args))
        ]
        args = [
            arg
            if i in smem or i in outside
            else pltpu.with_memory_space_constraint(arg, pltpu.VMEM)
            for i, arg in enumerate(args)
        ]
        outs = out_shape if isinstance(out_shape, (list, tuple)) else None
        out_specs = (
            [pl.BlockSpec(memory_space=pltpu.VMEM)] * len(outs)
            if outs
            else pl.BlockSpec(memory_space=pltpu.VMEM)
        )
        return pl.pallas_call(
            kernel,
            out_shape=out_shape,
            in_specs=specs,
            out_specs=out_specs,
            scratch_shapes=list(scratch),
            name=kernel.__name__,
        )(*args)

    return run


def pack_kernel(lame, probes, material, own, to_y, to_z):
    odd = lax.axis_index("tile_2") == 1
    for z in range(OWN_Z):
        for x in range(OWN_X):
            for c in range(3):
                own[(z * OWN_X + x) * 3 + c] = probes[
                    pl.ds((c * OWN_Z + z) * OWN_X + x, PROBES, stride=ROWS), :
                ]
    fields = {}
    for z in range(OWN_Z):
        kinds = material[z]
        for k in range(2):
            value = jnp.where(
                kinds == 0, lame[k, 0], jnp.where(kinds == 1, lame[k, 1], lame[k, 2])
            )
            fields[k, z] = value * (1.0 / 16.0)
            own[48 + k * 2 + z] = fields[k, z]
    first_y = jnp.where(odd, 0, OWN_X - 2)
    first_z = jnp.where(odd, OWN_X - 2, 0)
    for first, to in ((first_y, to_y), (first_z, to_z)):
        for z in range(OWN_Z):
            for xx in range(2):
                for c in range(3):
                    to[(z * 2 + xx) * 3 + c] = own[(z * OWN_X + first + xx) * 3 + c]
    low = jnp.concatenate([fields[k, z][0:2] for k in range(2) for z in range(2)], 0)
    high = jnp.concatenate([fields[k, z][6:8] for k in range(2) for z in range(2)], 0)
    to_y[12] = jnp.where(odd, low, high)
    to_z[12] = jnp.where(odd, high, low)


def stress(modes, lam, mu):
    a, b, e, p, q, r, t = modes
    third = 1.0 / 3.0
    lam3 = lam * third
    mu3 = mu * third
    both = mu + lam3
    top = (4.0 * mu + lam) * (1.0 / 9.0)
    twice = mu + mu
    trace = lam * (a[0] + b[1] + e[2])
    s01 = mu * (b[0] + a[1])
    s02 = mu * (e[0] + a[2])
    s12 = mu * (e[1] + b[2])
    aa = (twice * a[0] + trace, s01, s02)
    bb = (s01, twice * b[1] + trace, s12)
    ee = (s02, s12, twice * e[2] + trace)
    mixed = p[2] + q[1] + r[0]
    pp = (both * p[0] + lam3 * r[2], both * p[1] + lam3 * q[2], mu3 * (p[2] + mixed))
    qq = (both * q[0] + lam3 * r[1], mu3 * (q[1] + mixed), both * q[2] + lam3 * p[1])
    rr = (mu3 * (r[0] + mixed), both * r[1] + lam3 * q[0], both * r[2] + lam3 * p[0])
    tt = tuple(top * t[c] for c in range(3))
    return aa, bb, ee, pp, qq, rr, tt


def along_x(values):
    s0, d0, s1, d1 = values
    return (s0 + s1, s1 - s0, d0 + d1, d1 - d0)


def element(lower, upper, lam, mu):
    modes = tuple(
        tuple(
            upper[c][kind] - lower[c][kind] if minus else upper[c][kind] + lower[c][kind]
            for c in range(3)
        )
        for kind, minus in (
            (0, True),
            (1, False),
            (2, False),
            (1, True),
            (2, True),
            (3, False),
            (3, True),
        )
    )
    return stress(modes, lam, mu)


def to_lower(duals, c):
    aa, bb, ee, pp, qq, rr, tt = duals
    return (-aa[c], bb[c] - pp[c], ee[c] - qq[c], rr[c] - tt[c])


def to_upper(duals, c):
    aa, bb, ee, pp, qq, rr, tt = duals
    return (aa[c], bb[c] + pp[c], ee[c] + qq[c], rr[c] + tt[c])


def edge_masks():
    lanes = lax.broadcasted_iota(jnp.int32, (8, SPAN), 1)
    not_last = jnp.where(lanes == SPAN - 1, 0.0, 1.0).astype(F32)
    not_first = jnp.where(lanes == 0, 0.0, 1.0).astype(F32)
    return not_last, not_first

def spread(value, not_last):
    after = pltpu.roll(value, SPAN - 1, 1) * not_last
    return value + after, after - value


class Column:
    def __init__(self, not_first):
        self.not_first = not_first
        self.left = {}

    def node(self, key, parts):
        ss, ds, sd, dd = parts
        now_s, now_d = ss - ds, sd - dd
        if key in self.left:
            now_s = now_s + self.left[key][0]
            now_d = now_d + self.left[key][1]
        self.left[key] = (ss + ds, sd + dd)
        return (now_s - now_d) + pltpu.roll(now_s + now_d, 1, 1) * self.not_first


def nodes_of(ref, x, c, sign=None):
    at = (x * 3 + c) * 2
    values = (ref[at], ref[at + 1], ref[at + 6], ref[at + 7])
    if sign is not None and c == 0:
        values = tuple(sign * value for value in values)
    return along_x(values)


def layer_of(ref, x, sign=None):
    return [nodes_of(ref, x, c, sign) for c in range(3)]


def moduli(rows, x):
    return tuple(jnp.broadcast_to(rows[at : at + 1, :], (8, SPAN)) for at in (x, 16 + x))


def inner_kernel(
    own, from_y, from_z, pairs_a, pairs_b, base_a, base_b, rows, to_a, to_b, probes_block
):
    odd = lax.axis_index("tile_2") == 1
    first_core = lax.axis_index("layer_1") == 0
    sign = jnp.where(first_core, -1.0, 1.0).astype(F32)
    not_last, not_first = edge_masks()
    for x in range(WIDE_X):
        for c in range(3):
            values = []
            for z in range(OWN_Z):
                if x < 2:
                    at = (z * 2 + x) * 3 + c
                    values.append(jnp.where(odd, from_y[at], from_z[at]))
                elif x < 10:
                    values.append(own[(z * OWN_X + x - 2) * 3 + c])
                else:
                    at = (z * 2 + x - 10) * 3 + c
                    values.append(jnp.where(odd, from_z[at], from_y[at]))
            near_a = jnp.where(first_core, values[1], values[0])
            near_b = jnp.where(first_core, values[0], values[1])
            to_a[x * 3 + c] = near_a
            to_b[x * 3 + c] = near_b
            for half, pairs, value in ((0, pairs_a, near_a), (1, pairs_b, near_b)):
                pairs[(x * 3 + c) * 2], pairs[(x * 3 + c) * 2 + 1] = spread(value, not_last)
                if 2 <= x < 10:
                    at = (half * HALF + (x - 2) * 3 + c) * SPAN
                    probes_block[:, at : at + SPAN] = value
    left = jnp.where(odd, from_y[12], from_z[12])
    right = jnp.where(odd, from_z[12], from_y[12])
    for z in range(OWN_Z):
        for k in range(2):
            at = (z * 2 + k) * 16
            rows[at + 2 : at + 10, :] = own[48 + k * 2 + z]
            rows[at : at + 2, :] = left[k * 4 + z * 2 : k * 4 + z * 2 + 2]
            rows[at + 10 : at + 12, :] = right[k * 4 + z * 2 : k * 4 + z * 2 + 2]
            rows[at + 12 : at + 16, :] = jnp.zeros((4, SPAN), F32)
    for i in range(4):
        first, second = rows[i * 8 : i * 8 + 8, :], rows[32 + i * 8 : 40 + i * 8, :]
        to_a[66 + i] = jnp.where(first_core, second, first)
        to_b[66 + i] = jnp.where(first_core, first, second)
    column = Column(not_first)
    for x in range(WIDE_X - 1):
        duals = element(layer_of(pairs_a, x, sign), layer_of(pairs_b, x, sign), *moduli(rows, x))
        for c in range(3):
            force_a = column.node((0, c), to_lower(duals, c))
            force_b = column.node((1, c), to_upper(duals, c))
            if x:
                if c == 0:
                    force_a, force_b = sign * force_a, sign * force_b
                base_a[x * 3 + c] = force_a
                base_b[x * 3 + c] = force_b
                to_a[33 + x * 3 + c] = force_a
                to_b[33 + x * 3 + c] = force_b


def side_pass(above, other, pairs, base, rows, pairs_other, rows_side, near_one, far_one, one_block, first):
    tile = (lax.axis_index("tile_0") * 16 + lax.axis_index("tile_1")) * 2 + lax.axis_index("tile_2")
    layer = lax.axis_index("layer_0") * 2 + lax.axis_index("layer_1")
    not_last, not_first = edge_masks()
    sign = jnp.where(above, 1.0, -1.0).astype(F32)
    keep_x = jnp.where(tile == 127, 0.0, 1.0).astype(F32)
    keep_z = jnp.where((layer == 3) & above, 0.0, 1.0).astype(F32)
    for x in range(WIDE_X):
        for c in range(3):
            at = (x * 3 + c) * 2
            pairs_other[at], pairs_other[at + 1] = spread(other[x * 3 + c], not_last)
    for i in range(4):
        rows_side[i * 8 : i * 8 + 8, :] = jnp.where(
            above, rows[32 + i * 8 : 40 + i * 8, :], other[66 + i]
        )
    column = Column(not_first)
    for x in range(WIDE_X - 1):
        duals = element(
            layer_of(pairs, x, sign), layer_of(pairs_other, x, sign), *moduli(rows_side, x)
        )
        for c in range(3):
            near = column.node((0, c), to_lower(duals, c))
            far = column.node((1, c), to_upper(duals, c))
            if x:
                if c == 0:
                    near, far = sign * near, sign * far
                near = near + base[x * 3 + c]
                far = (far + other[33 + x * 3 + c]) * keep_z
                if x == 10:
                    near, far = near * keep_x, far * keep_x
                if 2 <= x < 10:
                    at = (first + (x - 2) * 3 + c) * SPAN
                    one_block[:, at : at + SPAN] = near
                at = (x * 3 + c) * 2
                near_one[at], near_one[at + 1] = spread(near, not_last)
                far_one[at], far_one[at + 1] = spread(far, not_last)
    return sign


def side_a_kernel(
    other, pairs, base, rows, near_one, one_block, two_side, pairs_other, rows_side, far_one
):
    above = lax.axis_index("layer_1") == 0
    sign = side_pass(
        above, other, pairs, base, rows, pairs_other, rows_side, near_one, far_one, one_block, 0
    )
    column = Column(edge_masks()[1])
    for x in range(1, WIDE_X - 2):
        duals = element(
            layer_of(near_one, x, sign), layer_of(far_one, x, sign), *moduli(rows_side, x)
        )
        for c in range(3):
            force = column.node(c, to_lower(duals, c))
            if x > 1:
                two_side[(x - 2) * 3 + c] = sign * force if c == 0 else force


def side_b_kernel(
    other,
    pairs,
    base,
    rows,
    near_a,
    one_block_a,
    two_a,
    probes_block,
    block,
    message,
    pairs_other,
    rows_side,
    near_one,
    far_one,
    one_block,
):
    above = lax.axis_index("layer_1") == 1
    block[0:8, :] = probes_block[...]
    block[8:16, 0 : HALF * SPAN] = one_block_a[...]
    sign = side_pass(
        above, other, pairs, base, rows, pairs_other, rows_side, near_one, far_one, one_block, 0
    )
    block[8:16, HALF * SPAN :] = one_block[...]
    column = Column(edge_masks()[1])
    for x in range(1, WIDE_X - 2):
        outer = element(
            layer_of(near_one, x, sign), layer_of(far_one, x, sign), *moduli(rows_side, x)
        )
        inner = element(layer_of(near_a, x, sign), layer_of(near_one, x, sign), *moduli(rows, x))
        for c in range(3):
            both = zip(to_lower(outer, c), to_upper(inner, c))
            force_b = column.node((1, c), tuple(one + two for one, two in both))
            force_a = column.node((0, c), to_lower(inner, c))
            if x > 1:
                if c == 0:
                    force_a, force_b = sign * force_a, sign * force_b
                at = ((x - 2) * 3 + c) * SPAN
                block[16:24, at : at + SPAN] = force_a + two_a[(x - 2) * 3 + c]
                at = at + HALF * SPAN
                block[16:24, at : at + SPAN] = force_b
    every = block[...]
    grams = lax.dot_general(
        every[0:16], every, (((1,), (1,)), ((), ())), precision=HIGHEST, preferred_element_type=F32
    )
    lanes = lax.broadcasted_iota(jnp.int32, (8, SPAN), 1)
    wide = jnp.concatenate([grams, jnp.zeros((16, SPAN - 24), F32)], 1)
    packed = jnp.where(lanes < 16, wide[0:8], pltpu.roll(wide[8:16], 8, 1))
    for i in range(message.shape[0]):
        message[i] = packed


def total_kernel(parts, message):
    total = parts[0]
    for i in range(1, parts.shape[0]):
        total = total + parts[i]
    for i in range(message.shape[0]):
        message[i] = total


def eliminate(table, first):
    rows = lax.broadcasted_iota(jnp.int32, (8, SPAN), 0)
    for k in range(8):
        pivot_row = jnp.broadcast_to(table[k : k + 1, :], (8, SPAN))
        column = jnp.broadcast_to(table[:, first + k : first + k + 1], (8, SPAN))
        pivot = jnp.broadcast_to(table[k : k + 1, first + k : first + k + 1], (8, SPAN))
        scaled = pivot_row / pivot
        table = jnp.where(rows == k, scaled, table - column * scaled)
    return table


def times(left, first, right):
    total = None
    for k in range(8):
        column = jnp.broadcast_to(left[:, first + k : first + k + 1], (8, SPAN))
        row = jnp.broadcast_to(right[k : k + 1, :], (8, SPAN))
        total = column * row if total is None else total + column * row
    return total


def final_kernel(parts, block, solution_rows, residual_rows):
    table = parts[0]
    for i in range(1, parts.shape[0]):
        table = table + parts[i]
    lanes = lax.broadcasted_iota(jnp.int32, (8, SPAN), 1)
    solved = eliminate(table, 8)
    product = times(table, 16, solved)
    shifted = pltpu.roll(table, SPAN - 8, 1)
    second = jnp.where(lanes < 8, product - shifted, shifted - product)
    coef_c = jnp.where(lanes < 8, eliminate(second, 16), 0.0)
    coef_b = jnp.where(lanes < 8, solved + times(solved, 16, coef_c), 0.0)
    coefs = jnp.concatenate(
        [coef_b, -coef_c - pltpu.roll(coef_b, 8, 1), pltpu.roll(coef_c, 8, 1)], 0
    )[:, 0:16]
    every = block[...]
    mixed = lax.dot_general(
        coefs, every, (((0,), (0,)), ((), ())), precision=HIGHEST, preferred_element_type=F32
    )
    first_core = lax.axis_index("layer_1") == 0
    for half in range(2):
        layer = jnp.where(first_core, 1 - half, half)
        for x in range(OWN_X):
            for c in range(3):
                at = (half * HALF + x * 3 + c) * SPAN
                rows = pl.ds((c * OWN_Z + layer) * OWN_X + x, PROBES, stride=ROWS)
                solution_rows[rows, :] = mixed[0:8, at : at + SPAN]
                residual_rows[rows, :] = every[0:8, at : at + SPAN] + mixed[8:16, at : at + SPAN]


def body(probes, material, lame_pairs):
    tiles = lax.axis_size(TILE)
    in_y = [(i, i ^ 1) for i in range(tiles)]
    in_z = [(i, ((i + 1) ^ 1) - 1) for i in range(1, tiles - 1)]
    in_core = [(0, 1), (1, 0), (2, 3), (3, 2)]
    in_chip = [(1, 2), (2, 1)]
    own, to_y, to_z = call(pack_kernel, (vregs(52), vregs(EDGE), vregs(EDGE)), smem=(0,), outside=(1, 2))(
        lame_pairs.T, probes.reshape(PROBES * ROWS, SPAN), material
    )
    from_z = lax.ppermute(to_z, TILE, in_z)
    from_y = lax.ppermute(to_y, TILE, in_y)
    moduli_rows = pltpu.VMEM((64, SPAN), F32)
    half_block = pltpu.VMEM((8, HALF * SPAN), F32)
    pairs_a, pairs_b, base_a, base_b, rows, to_a, to_b, probes_block = call(
        inner_kernel,
        (
            vregs(SIDE),
            vregs(SIDE),
            vregs(36),
            vregs(36),
            moduli_rows,
            vregs(FULL),
            vregs(FULL),
            pltpu.VMEM((8, 2 * HALF * SPAN), F32),
        ),
    )(own, from_y, from_z)
    from_b = lax.ppermute(to_b, LAYER, in_chip)
    from_a = lax.ppermute(to_a, LAYER, in_core)
    planes = lax.axis_size(PLANE)
    columns = lax.axis_size(COLUMN)
    scratch = (pltpu.VMEM((SIDE, 8, SPAN), F32), pltpu.VMEM((32, SPAN), F32))
    near_a, one_block_a, two_a = call(
        side_a_kernel,
        (vregs(SIDE), half_block, vregs(HALF)),
        scratch=(*scratch, pltpu.VMEM((SIDE, 8, SPAN), F32)),
    )(from_a, pairs_a, base_a, rows)
    block, message = call(
        side_b_kernel,
        (pltpu.VMEM((24, 2 * HALF * SPAN), F32), vregs(planes)),
        scratch=(
            *scratch,
            pltpu.VMEM((SIDE, 8, SPAN), F32),
            pltpu.VMEM((SIDE, 8, SPAN), F32),
            half_block,
        ),
    )(from_b, pairs_b, base_b, rows, near_a, one_block_a, two_a, probes_block)
    parts = lax.all_to_all(message, PLANE, 0, 0, tiled=True)
    message = call(total_kernel, vregs(columns))(parts)
    parts = lax.all_to_all(message, COLUMN, 0, 0, tiled=True)
    rows = jax.ShapeDtypeStruct((PROBES * ROWS, SPAN), F32)
    solution_rows, residual_rows = call(final_kernel, (rows, rows))(parts, block)
    return solution_rows.reshape(probes.shape), residual_rows.reshape(probes.shape)


def solution(mesh):
    split = Mesh(
        mesh.devices.reshape(4, 16, 2, 2, 2), ("tile_0", "tile_1", "tile_2", "layer_0", "layer_1")
    )
    spread = P(None, None, LAYER, TILE, None)
    return jax.shard_map(
        body,
        mesh=split,
        in_specs=(spread, P(LAYER, TILE, None), P()),
        out_specs=(spread, spread),
        check_vma=False,
    )
```

```python
import jax
import jax.numpy as jnp
from jax import lax
from jax.experimental import pallas as pl
from jax.experimental.pallas import tpu as pltpu
from jax.sharding import Mesh
from jax.sharding import PartitionSpec as P


TILE = ("tile_0", "tile_1", "tile_2")
LAYER = ("layer_0", "layer_1")
PLANE = ("tile_0", "tile_2", "layer_0", "layer_1")
COLUMN = "tile_1"

PROBES = 8
OWN_Z = 2
OWN_X = 8
WIDE_X = OWN_X + 4
SPAN = 128
ROWS = 3 * OWN_Z * OWN_X
EDGE = 13
FULL = 70
SIDE = 6 * WIDE_X
HALF = 3 * OWN_X
F32 = jnp.float32
HIGHEST = lax.Precision.HIGHEST


def vregs(*shape):
    return pltpu.VMEM((*shape, 8, SPAN), F32)


def call(kernel, out_shape, scratch=(), smem=(), outside=()):
    def run(*args):
        specs = [
            pl.BlockSpec(memory_space=pltpu.SMEM if i in smem else pltpu.VMEM)
            for i in range(len(args))
        ]
        args = [
            arg
            if i in smem or i in outside
            else pltpu.with_memory_space_constraint(arg, pltpu.VMEM)
            for i, arg in enumerate(args)
        ]
        outs = out_shape if isinstance(out_shape, (list, tuple)) else None
        out_specs = (
            [pl.BlockSpec(memory_space=pltpu.VMEM)] * len(outs)
            if outs
            else pl.BlockSpec(memory_space=pltpu.VMEM)
        )
        return pl.pallas_call(
            kernel,
            out_shape=out_shape,
            in_specs=specs,
            out_specs=out_specs,
            scratch_shapes=list(scratch),
        )(*args)

    return run


def pack_kernel(lame, probes, material, own, to_y, to_z):
    odd = lax.axis_index("tile_2") == 1
    for z in range(OWN_Z):
        for x in range(OWN_X):
            for c in range(3):
                own[(z * OWN_X + x) * 3 + c] = probes[
                    pl.ds((c * OWN_Z + z) * OWN_X + x, PROBES, stride=ROWS), :
                ]
    fields = {}
    for z in range(OWN_Z):
        kinds = material[z]
        for k in range(2):
            value = jnp.where(
                kinds == 0, lame[k, 0], jnp.where(kinds == 1, lame[k, 1], lame[k, 2])
            )
            fields[k, z] = value * (1.0 / 16.0)
            own[48 + k * 2 + z] = fields[k, z]
    first_y = jnp.where(odd, 0, OWN_X - 2)
    first_z = jnp.where(odd, OWN_X - 2, 0)
    for first, to in ((first_y, to_y), (first_z, to_z)):
        for z in range(OWN_Z):
            for xx in range(2):
                for c in range(3):
                    to[(z * 2 + xx) * 3 + c] = own[(z * OWN_X + first + xx) * 3 + c]
    low = jnp.concatenate([fields[k, z][0:2] for k in range(2) for z in range(2)], 0)
    high = jnp.concatenate([fields[k, z][6:8] for k in range(2) for z in range(2)], 0)
    to_y[12] = jnp.where(odd, low, high)
    to_z[12] = jnp.where(odd, high, low)


def stress(modes, lam, mu):
    a, b, e, p, q, r, t = modes
    third = 1.0 / 3.0
    lam3 = lam * third
    mu3 = mu * third
    both = mu + lam3
    top = (4.0 * mu + lam) * (1.0 / 9.0)
    twice = mu + mu
    trace = lam * (a[0] + b[1] + e[2])
    s01 = mu * (b[0] + a[1])
    s02 = mu * (e[0] + a[2])
    s12 = mu * (e[1] + b[2])
    aa = (twice * a[0] + trace, s01, s02)
    bb = (s01, twice * b[1] + trace, s12)
    ee = (s02, s12, twice * e[2] + trace)
    mixed = p[2] + q[1] + r[0]
    pp = (both * p[0] + lam3 * r[2], both * p[1] + lam3 * q[2], mu3 * (p[2] + mixed))
    qq = (both * q[0] + lam3 * r[1], mu3 * (q[1] + mixed), both * q[2] + lam3 * p[1])
    rr = (mu3 * (r[0] + mixed), both * r[1] + lam3 * q[0], both * r[2] + lam3 * p[0])
    tt = tuple(top * t[c] for c in range(3))
    return aa, bb, ee, pp, qq, rr, tt


def along_x(values):
    s0, d0, s1, d1 = values
    return (s0 + s1, s1 - s0, d0 + d1, d1 - d0)


def element(lower, upper, lam, mu):
    modes = tuple(
        tuple(
            upper[c][kind] - lower[c][kind] if minus else upper[c][kind] + lower[c][kind]
            for c in range(3)
        )
        for kind, minus in (
            (0, True),
            (1, False),
            (2, False),
            (1, True),
            (2, True),
            (3, False),
            (3, True),
        )
    )
    return stress(modes, lam, mu)


def to_lower(duals, c):
    aa, bb, ee, pp, qq, rr, tt = duals
    return (-aa[c], bb[c] - pp[c], ee[c] - qq[c], rr[c] - tt[c])


def to_upper(duals, c):
    aa, bb, ee, pp, qq, rr, tt = duals
    return (aa[c], bb[c] + pp[c], ee[c] + qq[c], rr[c] + tt[c])


def edge_masks():
    lanes = lax.broadcasted_iota(jnp.int32, (8, SPAN), 1)
    not_last = jnp.where(lanes == SPAN - 1, 0.0, 1.0).astype(F32)
    not_first = jnp.where(lanes == 0, 0.0, 1.0).astype(F32)
    return not_last, not_first


def spread(value, not_last):
    after = pltpu.roll(value, SPAN - 1, 1) * not_last
    return value + after, after - value


class Column:
    def __init__(self, not_first):
        self.not_first = not_first
        self.left = {}

    def node(self, key, parts):
        ss, ds, sd, dd = parts
        now_s, now_d = ss - ds, sd - dd
        if key in self.left:
            now_s = now_s + self.left[key][0]
            now_d = now_d + self.left[key][1]
        self.left[key] = (ss + ds, sd + dd)
        return (now_s - now_d) + pltpu.roll(now_s + now_d, 1, 1) * self.not_first


def nodes_of(ref, x, c, sign=None):
    at = (x * 3 + c) * 2
    values = (ref[at], ref[at + 1], ref[at + 6], ref[at + 7])
    if sign is not None and c == 0:
        values = tuple(sign * value for value in values)
    return along_x(values)


def layer_of(ref, x, sign=None):
    return [nodes_of(ref, x, c, sign) for c in range(3)]


def moduli(rows, x):
    return tuple(jnp.broadcast_to(rows[at : at + 1, :], (8, SPAN)) for at in (x, 16 + x))


def inner_kernel(
    own, from_y, from_z, pairs_a, pairs_b, base_a, base_b, rows, to_a, to_b, probes_block
):
    odd = lax.axis_index("tile_2") == 1
    first_core = lax.axis_index("layer_1") == 0
    sign = jnp.where(first_core, -1.0, 1.0).astype(F32)
    not_last, not_first = edge_masks()
    for x in range(WIDE_X):
        for c in range(3):
            values = []
            for z in range(OWN_Z):
                if x < 2:
                    at = (z * 2 + x) * 3 + c
                    values.append(jnp.where(odd, from_y[at], from_z[at]))
                elif x < 10:
                    values.append(own[(z * OWN_X + x - 2) * 3 + c])
                else:
                    at = (z * 2 + x - 10) * 3 + c
                    values.append(jnp.where(odd, from_z[at], from_y[at]))
            near_a = jnp.where(first_core, values[1], values[0])
            near_b = jnp.where(first_core, values[0], values[1])
            to_a[x * 3 + c] = near_a
            to_b[x * 3 + c] = near_b
            for half, pairs, value in ((0, pairs_a, near_a), (1, pairs_b, near_b)):
                pairs[(x * 3 + c) * 2], pairs[(x * 3 + c) * 2 + 1] = spread(value, not_last)
                if 2 <= x < 10:
                    at = (half * HALF + (x - 2) * 3 + c) * SPAN
                    probes_block[:, at : at + SPAN] = value
    left = jnp.where(odd, from_y[12], from_z[12])
    right = jnp.where(odd, from_z[12], from_y[12])
    for z in range(OWN_Z):
        for k in range(2):
            at = (z * 2 + k) * 16
            rows[at + 2 : at + 10, :] = own[48 + k * 2 + z]
            rows[at : at + 2, :] = left[k * 4 + z * 2 : k * 4 + z * 2 + 2]
            rows[at + 10 : at + 12, :] = right[k * 4 + z * 2 : k * 4 + z * 2 + 2]
            rows[at + 12 : at + 16, :] = jnp.zeros((4, SPAN), F32)
    for i in range(4):
        first, second = rows[i * 8 : i * 8 + 8, :], rows[32 + i * 8 : 40 + i * 8, :]
        to_a[66 + i] = jnp.where(first_core, second, first)
        to_b[66 + i] = jnp.where(first_core, first, second)
    column = Column(not_first)
    for x in range(WIDE_X - 1):
        duals = element(layer_of(pairs_a, x, sign), layer_of(pairs_b, x, sign), *moduli(rows, x))
        for c in range(3):
            force_a = column.node((0, c), to_lower(duals, c))
            force_b = column.node((1, c), to_upper(duals, c))
            if x:
                if c == 0:
                    force_a, force_b = sign * force_a, sign * force_b
                base_a[x * 3 + c] = force_a
                base_b[x * 3 + c] = force_b
                to_a[33 + x * 3 + c] = force_a
                to_b[33 + x * 3 + c] = force_b


def side_pass(above, other, pairs, base, rows, pairs_other, rows_side, near_one, far_one, one_block, first):
    tile = (lax.axis_index("tile_0") * 16 + lax.axis_index("tile_1")) * 2 + lax.axis_index("tile_2")
    layer = lax.axis_index("layer_0") * 2 + lax.axis_index("layer_1")
    not_last, not_first = edge_masks()
    sign = jnp.where(above, 1.0, -1.0).astype(F32)
    keep_x = jnp.where(tile == 127, 0.0, 1.0).astype(F32)
    keep_z = jnp.where((layer == 3) & above, 0.0, 1.0).astype(F32)
    for x in range(WIDE_X):
        for c in range(3):
            at = (x * 3 + c) * 2
            pairs_other[at], pairs_other[at + 1] = spread(other[x * 3 + c], not_last)
    for i in range(4):
        rows_side[i * 8 : i * 8 + 8, :] = jnp.where(
            above, rows[32 + i * 8 : 40 + i * 8, :], other[66 + i]
        )
    column = Column(not_first)
    for x in range(WIDE_X - 1):
        duals = element(
            layer_of(pairs, x, sign), layer_of(pairs_other, x, sign), *moduli(rows_side, x)
        )
        for c in range(3):
            near = column.node((0, c), to_lower(duals, c))
            far = column.node((1, c), to_upper(duals, c))
            if x:
                if c == 0:
                    near, far = sign * near, sign * far
                near = near + base[x * 3 + c]
                far = (far + other[33 + x * 3 + c]) * keep_z
                if x == 10:
                    near, far = near * keep_x, far * keep_x
                if 2 <= x < 10:
                    at = (first + (x - 2) * 3 + c) * SPAN
                    one_block[:, at : at + SPAN] = near
                at = (x * 3 + c) * 2
                near_one[at], near_one[at + 1] = spread(near, not_last)
                far_one[at], far_one[at + 1] = spread(far, not_last)
    return sign


def side_a_kernel(
    other, pairs, base, rows, near_one, one_block, two_side, pairs_other, rows_side, far_one
):
    above = lax.axis_index("layer_1") == 0
    sign = side_pass(
        above, other, pairs, base, rows, pairs_other, rows_side, near_one, far_one, one_block, 0
    )
    column = Column(edge_masks()[1])
    for x in range(1, WIDE_X - 2):
        duals = element(
            layer_of(near_one, x, sign), layer_of(far_one, x, sign), *moduli(rows_side, x)
        )
        for c in range(3):
            force = column.node(c, to_lower(duals, c))
            if x > 1:
                two_side[(x - 2) * 3 + c] = sign * force if c == 0 else force


def side_b_kernel(
    other,
    pairs,
    base,
    rows,
    near_a,
    one_block_a,
    two_a,
    probes_block,
    block,
    message,
    pairs_other,
    rows_side,
    near_one,
    far_one,
    one_block,
):
    above = lax.axis_index("layer_1") == 1
    block[0:8, :] = probes_block[...]
    block[8:16, 0 : HALF * SPAN] = one_block_a[...]
    sign = side_pass(
        above, other, pairs, base, rows, pairs_other, rows_side, near_one, far_one, one_block, 0
    )
    block[8:16, HALF * SPAN :] = one_block[...]
    column = Column(edge_masks()[1])
    for x in range(1, WIDE_X - 2):
        outer = element(
            layer_of(near_one, x, sign), layer_of(far_one, x, sign), *moduli(rows_side, x)
        )
        inner = element(layer_of(near_a, x, sign), layer_of(near_one, x, sign), *moduli(rows, x))
        for c in range(3):
            both = zip(to_lower(outer, c), to_upper(inner, c))
            force_b = column.node((1, c), tuple(one + two for one, two in both))
            force_a = column.node((0, c), to_lower(inner, c))
            if x > 1:
                if c == 0:
                    force_a, force_b = sign * force_a, sign * force_b
                at = ((x - 2) * 3 + c) * SPAN
                block[16:24, at : at + SPAN] = force_a + two_a[(x - 2) * 3 + c]
                at = at + HALF * SPAN
                block[16:24, at : at + SPAN] = force_b
    every = block[...]
    grams = lax.dot_general(
        every[0:16], every, (((1,), (1,)), ((), ())), precision=HIGHEST, preferred_element_type=F32
    )
    lanes = lax.broadcasted_iota(jnp.int32, (8, SPAN), 1)
    wide = jnp.concatenate([grams, jnp.zeros((16, SPAN - 24), F32)], 1)
    packed = jnp.where(lanes < 16, wide[0:8], pltpu.roll(wide[8:16], 8, 1))
    packed = turned(jnp.where(lanes < 32, packed, 0.0), 1)
    halves = [packed[i : i + 1] + packed[i + 1 : i + 2] for i in (0, 2, 4, 6)]
    packed = jnp.concatenate([halves[0] + halves[1], halves[2] + halves[3]], 0)
    for i in range(message.shape[0]):
        message[i] = packed


def turned(table, way):
    quarter = lax.broadcasted_iota(jnp.int32, (8, SPAN), 0) & 3
    result = table
    for i in range(1, 4):
        result = jnp.where(quarter == i, pltpu.roll(table, (way * 32 * i) % SPAN, 1), result)
    return result


def total_kernel(parts, message):
    total = parts[0]
    for i in range(1, parts.shape[0]):
        total = total + parts[i]
    for i in range(message.shape[0]):
        message[i] = total


def eliminate(table, first):
    rows = lax.broadcasted_iota(jnp.int32, (8, SPAN), 0)
    for k in range(0, 8, 2):
        top = jnp.broadcast_to(table[k : k + 1, :], (8, SPAN))
        low = jnp.broadcast_to(table[k + 1 : k + 2, :], (8, SPAN))
        left = jnp.broadcast_to(table[:, first + k : first + k + 1], (8, SPAN))
        right = jnp.broadcast_to(table[:, first + k + 1 : first + k + 2], (8, SPAN))
        p00 = jnp.broadcast_to(left[k : k + 1, :], (8, SPAN))
        p10 = jnp.broadcast_to(left[k + 1 : k + 2, :], (8, SPAN))
        p01 = jnp.broadcast_to(right[k : k + 1, :], (8, SPAN))
        p11 = jnp.broadcast_to(right[k + 1 : k + 2, :], (8, SPAN))
        scale = 1.0 / (p00 * p11 - p01 * p10)
        new_top = (p11 * top - p01 * low) * scale
        new_low = (p00 * low - p10 * top) * scale
        rest = table - left * new_top - right * new_low
        table = jnp.where(rows == k, new_top, jnp.where(rows == k + 1, new_low, rest))
    return table


def times(left, first, right):
    total = None
    for k in range(8):
        column = jnp.broadcast_to(left[:, first + k : first + k + 1], (8, SPAN))
        row = jnp.broadcast_to(right[k : k + 1, :], (8, SPAN))
        total = column * row if total is None else total + column * row
    return total


def final_kernel(parts, block, solution_rows, residual_rows):
    total = parts[0]
    for i in range(1, parts.shape[0]):
        total = total + parts[i]
    lanes = lax.broadcasted_iota(jnp.int32, (8, SPAN), 1)
    table = jnp.concatenate([jnp.broadcast_to(total[i : i + 1], (4, SPAN)) for i in (0, 1)], 0)
    table = jnp.where(lanes < 32, turned(table, -1), 0.0)
    solved = eliminate(table, 8)
    product = times(table, 16, solved)
    shifted = pltpu.roll(table, SPAN - 8, 1)
    second = jnp.where(lanes < 8, product - shifted, shifted - product)
    coef_c = jnp.where(lanes < 8, eliminate(second, 16), 0.0)
    coef_b = jnp.where(lanes < 8, solved + times(solved, 16, coef_c), 0.0)
    coefs = jnp.concatenate(
        [coef_b, -coef_c - pltpu.roll(coef_b, 8, 1), pltpu.roll(coef_c, 8, 1)], 0
    )[:, 0:16]
    every = block[...]
    mixed = lax.dot_general(
        coefs, every, (((0,), (0,)), ((), ())), precision=HIGHEST, preferred_element_type=F32
    )
    first_core = lax.axis_index("layer_1") == 0
    for half in range(2):
        layer = jnp.where(first_core, 1 - half, half)
        for x in range(OWN_X):
            for c in range(3):
                at = (half * HALF + x * 3 + c) * SPAN
                rows = pl.ds((c * OWN_Z + layer) * OWN_X + x, PROBES, stride=ROWS)
                solution_rows[rows, :] = mixed[0:8, at : at + SPAN]
                residual_rows[rows, :] = every[0:8, at : at + SPAN] + mixed[8:16, at : at + SPAN]


def body(probes, material, lame_pairs):
    tiles = lax.axis_size(TILE)
    in_y = [(i, i ^ 1) for i in range(tiles)]
    in_z = [(i, ((i + 1) ^ 1) - 1) for i in range(1, tiles - 1)]
    in_core = [(0, 1), (1, 0), (2, 3), (3, 2)]
    in_chip = [(1, 2), (2, 1)]
    own, to_y, to_z = call(pack_kernel, (vregs(52), vregs(EDGE), vregs(EDGE)), smem=(0,), outside=(1, 2))(
        lame_pairs.T, probes.reshape(PROBES * ROWS, SPAN), material
    )
    from_z = lax.ppermute(to_z, TILE, in_z)
    from_y = lax.ppermute(to_y, TILE, in_y)
    moduli_rows = pltpu.VMEM((64, SPAN), F32)
    half_block = pltpu.VMEM((8, HALF * SPAN), F32)
    pairs_a, pairs_b, base_a, base_b, rows, to_a, to_b, probes_block = call(
        inner_kernel,
        (
            vregs(SIDE),
            vregs(SIDE),
            vregs(36),
            vregs(36),
            moduli_rows,
            vregs(FULL),
            vregs(FULL),
            pltpu.VMEM((8, 2 * HALF * SPAN), F32),
        ),
    )(own, from_y, from_z)
    from_b = lax.ppermute(to_b, LAYER, in_chip)
    from_a = lax.ppermute(to_a, LAYER, in_core)
    planes = lax.axis_size(PLANE)
    columns = lax.axis_size(COLUMN)
    scratch = (pltpu.VMEM((SIDE, 8, SPAN), F32), pltpu.VMEM((32, SPAN), F32))
    near_a, one_block_a, two_a = call(
        side_a_kernel,
        (vregs(SIDE), half_block, vregs(HALF)),
        scratch=(*scratch, pltpu.VMEM((SIDE, 8, SPAN), F32)),
    )(from_a, pairs_a, base_a, rows)
    block, message = call(
        side_b_kernel,
        (pltpu.VMEM((24, 2 * HALF * SPAN), F32), pltpu.VMEM((planes, 2, SPAN), F32)),
        scratch=(
            *scratch,
            pltpu.VMEM((SIDE, 8, SPAN), F32),
            pltpu.VMEM((SIDE, 8, SPAN), F32),
            half_block,
        ),
    )(from_b, pairs_b, base_b, rows, near_a, one_block_a, two_a, probes_block)
    parts = lax.all_to_all(message, PLANE, 0, 0, tiled=True)
    message = call(total_kernel, pltpu.VMEM((columns, 2, SPAN), F32))(parts)
    parts = lax.all_to_all(message, COLUMN, 0, 0, tiled=True)
    rows = jax.ShapeDtypeStruct((PROBES * ROWS, SPAN), F32)
    solution_rows, residual_rows = call(final_kernel, (rows, rows))(parts, block)
    return solution_rows.reshape(probes.shape), residual_rows.reshape(probes.shape)


def solution(mesh):
    split = Mesh(
        mesh.devices.reshape(4, 16, 2, 2, 2), ("tile_0", "tile_1", "tile_2", "layer_0", "layer_1")
    )
    spread = P(None, None, LAYER, TILE, None)
    return jax.shard_map(
        body,
        mesh=split,
        in_specs=(spread, P(LAYER, TILE, None), P()),
        out_specs=(spread, spread),
        check_vma=False,
    )
```

```python
import jax
import jax.numpy as jnp
from jax import lax
from jax.experimental import pallas as pl
from jax.experimental.pallas import tpu as pltpu
from jax.sharding import Mesh
from jax.sharding import PartitionSpec as P


TILE = ("tile_0", "tile_1", "tile_2")
LAYER = ("layer_0", "layer_1")
PLANE = ("tile_0", "tile_2", "layer_0", "layer_1")
COLUMN = "tile_1"

PROBES = 8
OWN_Z = 2
OWN_X = 8
WIDE_X = OWN_X + 4
SPAN = 128
ROWS = 3 * OWN_Z * OWN_X
EDGE = 13
FULL = 70
SIDE = 6 * WIDE_X
HALF = 3 * OWN_X
F32 = jnp.float32
HIGHEST = lax.Precision.HIGHEST


def vregs(*shape):
    return pltpu.VMEM((*shape, 8, SPAN), F32)


def call(kernel, out_shape, scratch=(), smem=(), outside=(), aliases=None):
    def run(*args):
        specs = [
            pl.BlockSpec(memory_space=pltpu.SMEM if i in smem else pltpu.VMEM)
            for i in range(len(args))
        ]
        args = [
            arg
            if i in smem or i in outside
            else pltpu.with_memory_space_constraint(arg, pltpu.VMEM)
            for i, arg in enumerate(args)
        ]
        outs = out_shape if isinstance(out_shape, (list, tuple)) else None
        out_specs = (
            [pl.BlockSpec(memory_space=pltpu.VMEM)] * len(outs)
            if outs
            else pl.BlockSpec(memory_space=pltpu.VMEM)
        )
        return pl.pallas_call(
            kernel,
            out_shape=out_shape,
            in_specs=specs,
            out_specs=out_specs,
            scratch_shapes=list(scratch),
            input_output_aliases=aliases or {},
        )(*args)

    return run


def pack_kernel(lame, probes, material, own, to_y, to_z):
    odd = lax.axis_index("tile_2") == 1
    for z in range(OWN_Z):
        for x in range(OWN_X):
            for c in range(3):
                own[(z * OWN_X + x) * 3 + c] = probes[
                    pl.ds((c * OWN_Z + z) * OWN_X + x, PROBES, stride=ROWS), :
                ]
    fields = {}
    for z in range(OWN_Z):
        kinds = material[z]
        for k in range(2):
            value = jnp.where(
                kinds == 0, lame[k, 0], jnp.where(kinds == 1, lame[k, 1], lame[k, 2])
            )
            fields[k, z] = value * (1.0 / 16.0)
            own[48 + k * 2 + z] = fields[k, z]
    first_y = jnp.where(odd, 0, OWN_X - 2)
    first_z = jnp.where(odd, OWN_X - 2, 0)
    for first, to in ((first_y, to_y), (first_z, to_z)):
        for z in range(OWN_Z):
            for xx in range(2):
                for c in range(3):
                    to[(z * 2 + xx) * 3 + c] = own[(z * OWN_X + first + xx) * 3 + c]
    low = jnp.concatenate([fields[k, z][0:2] for k in range(2) for z in range(2)], 0)
    high = jnp.concatenate([fields[k, z][6:8] for k in range(2) for z in range(2)], 0)
    to_y[12] = jnp.where(odd, low, high)
    to_z[12] = jnp.where(odd, high, low)


def stress(modes, lam, mu):
    a, b, e, p, q, r, t = modes
    third = 1.0 / 3.0
    lam3 = lam * third
    mu3 = mu * third
    both = mu + lam3
    top = (4.0 * mu + lam) * (1.0 / 9.0)
    twice = mu + mu
    trace = lam * (a[0] + b[1] + e[2])
    s01 = mu * (b[0] + a[1])
    s02 = mu * (e[0] + a[2])
    s12 = mu * (e[1] + b[2])
    aa = (twice * a[0] + trace, s01, s02)
    bb = (s01, twice * b[1] + trace, s12)
    ee = (s02, s12, twice * e[2] + trace)
    mixed = p[2] + q[1] + r[0]
    pp = (both * p[0] + lam3 * r[2], both * p[1] + lam3 * q[2], mu3 * (p[2] + mixed))
    qq = (both * q[0] + lam3 * r[1], mu3 * (q[1] + mixed), both * q[2] + lam3 * p[1])
    rr = (mu3 * (r[0] + mixed), both * r[1] + lam3 * q[0], both * r[2] + lam3 * p[0])
    tt = tuple(top * t[c] for c in range(3))
    return aa, bb, ee, pp, qq, rr, tt


def along_x(values):
    s0, d0, s1, d1 = values
    return (s0 + s1, s1 - s0, d0 + d1, d1 - d0)


def element(lower, upper, lam, mu):
    modes = tuple(
        tuple(
            upper[c][kind] - lower[c][kind] if minus else upper[c][kind] + lower[c][kind]
            for c in range(3)
        )
        for kind, minus in (
            (0, True),
            (1, False),
            (2, False),
            (1, True),
            (2, True),
            (3, False),
            (3, True),
        )
    )
    return stress(modes, lam, mu)


def to_lower(duals, c):
    aa, bb, ee, pp, qq, rr, tt = duals
    return (-aa[c], bb[c] - pp[c], ee[c] - qq[c], rr[c] - tt[c])


def to_upper(duals, c):
    aa, bb, ee, pp, qq, rr, tt = duals
    return (aa[c], bb[c] + pp[c], ee[c] + qq[c], rr[c] + tt[c])


def edge_masks():
    lanes = lax.broadcasted_iota(jnp.int32, (8, SPAN), 1)
    not_last = jnp.where(lanes == SPAN - 1, 0.0, 1.0).astype(F32)
    not_first = jnp.where(lanes == 0, 0.0, 1.0).astype(F32)
    return not_last, not_first


def spread(value, not_last):
    after = pltpu.roll(value, SPAN - 1, 1) * not_last
    return value + after, after - value


class Column:
    def __init__(self, not_first):
        self.not_first = not_first
        self.left = {}

    def node(self, key, parts):
        ss, ds, sd, dd = parts
        force = self.close(key, ss - ds, sd - dd)
        self.left[key] = (ss + ds, sd + dd)
        return force

    def close(self, key, now_s, now_d):
        if key in self.left:
            now_s = now_s + self.left[key][0]
            now_d = now_d + self.left[key][1]
        return (now_s - now_d) + pltpu.roll(now_s + now_d, 1, 1) * self.not_first


def nodes_of(ref, x, c, sign=None):
    at = (x * 3 + c) * 2
    values = (ref[at], ref[at + 1], ref[at + 6], ref[at + 7])
    if sign is not None and c == 0:
        values = tuple(sign * value for value in values)
    return along_x(values)


def layer_of(ref, x, sign=None):
    return [nodes_of(ref, x, c, sign) for c in range(3)]


def moduli(rows, x):
    return tuple(jnp.broadcast_to(rows[at : at + 1, :], (8, SPAN)) for at in (x, 16 + x))


def pick(first_core, values):
    return (
        jnp.where(first_core, values[1], values[0]),
        jnp.where(first_core, values[0], values[1]),
    )


def early_kernel(
    own, pairs_a, pairs_b, base_a, base_b, to_a, to_b, rows, edge, norms
):
    first_core = lax.axis_index("layer_1") == 0
    sign = jnp.where(first_core, -1.0, 1.0).astype(F32)
    not_last, not_first = edge_masks()
    for x in range(2, 10):
        for c in range(3):
            values = [own[(z * OWN_X + x - 2) * 3 + c] for z in range(OWN_Z)]
            for to, pairs, value in zip(
                (to_a, to_b), (pairs_a, pairs_b), pick(first_core, values)
            ):
                to[x * 3 + c] = value
                pairs[(x * 3 + c) * 2], pairs[(x * 3 + c) * 2 + 1] = spread(value, not_last)
    for z in range(OWN_Z):
        for k in range(2):
            at = (z * 2 + k) * 16
            rows[at : at + 16, :] = jnp.zeros((16, SPAN), F32)
            rows[at + 2 : at + 10, :] = own[48 + k * 2 + z]
    column = Column(not_first)
    for x in range(2, 9):
        duals = element(layer_of(pairs_a, x, sign), layer_of(pairs_b, x, sign), *moduli(rows, x))
        for c in range(3):
            for side, parts in ((0, to_lower(duals, c)), (1, to_upper(duals, c))):
                if x == 2:
                    at = (side * 3 + c) * 2
                    edge[at] = parts[0] - parts[1]
                    edge[at + 1] = parts[2] - parts[3]
                force = column.node((side, c), parts)
                if x > 2:
                    put(side, x, c, sign, force, (base_a, base_b), (to_a, to_b))
    for side in range(2):
        for c in range(3):
            at = 12 + (side * 3 + c) * 2
            edge[at], edge[at + 1] = column.left[side, c]
    for to in (to_a, to_b):
        for x in (0, 1, 10, 11):
            for c in range(3):
                to[x * 3 + c] = jnp.zeros((8, SPAN), F32)
    every = jnp.concatenate([own[i] for i in range(2 * HALF)], 1)
    gram = lax.dot_general(
        every, every, (((1,), (1,)), ((), ())), precision=HIGHEST, preferred_element_type=F32
    )
    norms[...] = jnp.concatenate([gram, jnp.zeros((8, SPAN - 8), F32)], 1)


def put(side, x, c, sign, force, bases, messages):
    force = sign * force if c == 0 else force
    bases[side][x * 3 + c] = force
    messages[side][33 + x * 3 + c] = force


def inner_kernel(
    from_y,
    from_z,
    edge,
    in_pairs_a,
    in_pairs_b,
    in_base_a,
    in_base_b,
    in_to_a,
    in_to_b,
    in_rows,
    pairs_a,
    pairs_b,
    base_a,
    base_b,
    to_a,
    to_b,
    rows,
    probes_block,
):
    odd = lax.axis_index("tile_2") == 1
    first_core = lax.axis_index("layer_1") == 0
    sign = jnp.where(first_core, -1.0, 1.0).astype(F32)
    not_last, not_first = edge_masks()
    for half, source in ((0, in_to_a), (1, in_to_b)):
        for i in range(HALF):
            at = (half * HALF + i) * SPAN
            probes_block[:, at : at + SPAN] = source[6 + i]
    fresh = {}
    for x in (0, 1, 10, 11):
        for c in range(3):
            values = []
            for z in range(OWN_Z):
                at = (z * 2 + x % 10) * 3 + c
                one, two = from_y[at], from_z[at]
                values.append(jnp.where(odd, one, two) if x < 2 else jnp.where(odd, two, one))
            for side, to, pairs, value in zip(
                (0, 1), (to_a, to_b), (pairs_a, pairs_b), pick(first_core, values)
            ):
                to[x * 3 + c] = value
                fresh[side, x, c] = spread(value, not_last)
                at = (x * 3 + c) * 2
                pairs[at], pairs[at + 1] = fresh[side, x, c]
    left = jnp.where(odd, from_y[12], from_z[12])
    right = jnp.where(odd, from_z[12], from_y[12])
    fields = {}
    for z in range(OWN_Z):
        for k in range(2):
            at = (z * 2 + k) * 16
            row = k * 4 + z * 2
            rows[at : at + 2, :] = left[row : row + 2]
            rows[at + 10 : at + 12, :] = right[row : row + 2]
            whole = jnp.concatenate(
                [left[row : row + 2], in_rows[at + 2 : at + 10, :], right[row : row + 2]]
                + [jnp.zeros((4, SPAN), F32)],
                0,
            )
            fields[z, k] = whole
    for k in range(2):
        for i in range(2):
            one, two = pick(first_core, [fields[z, k][i * 8 : i * 8 + 8] for z in range(OWN_Z)])
            to_a[66 + k * 2 + i] = one
            to_b[66 + k * 2 + i] = two

    def layer(side, x):
        source = (in_pairs_a, in_pairs_b)[side]
        combined = []
        for c in range(3):
            values = ()
            for at in (x, x + 1):
                if 2 <= at < 10:
                    values += (source[(at * 3 + c) * 2], source[(at * 3 + c) * 2 + 1])
                else:
                    values += fresh[side, at, c]
            if c == 0:
                values = tuple(sign * value for value in values)
            combined.append(along_x(values))
        return combined

    bases, messages = (base_a, base_b), (to_a, to_b)
    column = Column(not_first)
    for x in (0, 1, 9, 10):
        if x == 9:
            for side in range(2):
                for c in range(3):
                    at = (side * 3 + c) * 2
                    force = column.close((side, c), edge[at], edge[at + 1])
                    put(side, 2, c, sign, force, bases, messages)
                    column.left[side, c] = (edge[12 + at], edge[12 + at + 1])
        lam, mu = (
            jnp.broadcast_to(fields[0, k][x : x + 1], (8, SPAN)) for k in range(2)
        )
        duals = element(layer(0, x), layer(1, x), lam, mu)
        for c in range(3):
            for side, parts in ((0, to_lower(duals, c)), (1, to_upper(duals, c))):
                force = column.node((side, c), parts)
                if x:
                    put(side, x, c, sign, force, bases, messages)


def side_pass(above, other, pairs, base, rows, pairs_other, rows_side, near_one, far_one, one_block, first):
    tile = (lax.axis_index("tile_0") * 16 + lax.axis_index("tile_1")) * 2 + lax.axis_index("tile_2")
    layer = lax.axis_index("layer_0") * 2 + lax.axis_index("layer_1")
    not_last, not_first = edge_masks()
    sign = jnp.where(above, 1.0, -1.0).astype(F32)
    keep_x = jnp.where(tile == 127, 0.0, 1.0).astype(F32)
    keep_z = jnp.where((layer == 3) & above, 0.0, 1.0).astype(F32)
    for x in range(WIDE_X):
        for c in range(3):
            at = (x * 3 + c) * 2
            pairs_other[at], pairs_other[at + 1] = spread(other[x * 3 + c], not_last)
    for i in range(4):
        rows_side[i * 8 : i * 8 + 8, :] = jnp.where(
            above, rows[32 + i * 8 : 40 + i * 8, :], other[66 + i]
        )
    column = Column(not_first)
    for x in range(WIDE_X - 1):
        duals = element(
            layer_of(pairs, x, sign), layer_of(pairs_other, x, sign), *moduli(rows_side, x)
        )
        for c in range(3):
            near = column.node((0, c), to_lower(duals, c))
            far = column.node((1, c), to_upper(duals, c))
            if x:
                if c == 0:
                    near, far = sign * near, sign * far
                near = near + base[x * 3 + c]
                far = (far + other[33 + x * 3 + c]) * keep_z
                if x == 10:
                    near, far = near * keep_x, far * keep_x
                if 2 <= x < 10:
                    at = (first + (x - 2) * 3 + c) * SPAN
                    one_block[:, at : at + SPAN] = near
                at = (x * 3 + c) * 2
                near_one[at], near_one[at + 1] = spread(near, not_last)
                far_one[at], far_one[at + 1] = spread(far, not_last)
    return sign


def thirds(values):
    high = values.astype(jnp.bfloat16)
    rest = values - high.astype(F32)
    middle = rest.astype(jnp.bfloat16)
    low = (rest - middle.astype(F32)).astype(jnp.bfloat16)
    return high, middle, low


def side_a_kernel(
    other, pairs, base, rows, near_one, one_block, two_side, pairs_other, rows_side, far_one
):
    above = lax.axis_index("layer_1") == 0
    sign = side_pass(
        above, other, pairs, base, rows, pairs_other, rows_side, near_one, far_one, one_block, 0
    )
    column = Column(edge_masks()[1])
    for x in range(1, WIDE_X - 2):
        duals = element(
            layer_of(near_one, x, sign), layer_of(far_one, x, sign), *moduli(rows_side, x)
        )
        for c in range(3):
            force = column.node(c, to_lower(duals, c))
            if x > 1:
                two_side[(x - 2) * 3 + c] = sign * force if c == 0 else force


def side_b_kernel(
    other,
    pairs,
    base,
    rows,
    near_a,
    one_block_a,
    two_a,
    probes_block,
    norms,
    block,
    message,
    pairs_other,
    rows_side,
    near_one,
    far_one,
    one_block,
):
    above = lax.axis_index("layer_1") == 1
    block[0:8, :] = probes_block[...]
    block[8:16, 0 : HALF * SPAN] = one_block_a[...]
    sign = side_pass(
        above, other, pairs, base, rows, pairs_other, rows_side, near_one, far_one, one_block, 0
    )
    block[8:16, HALF * SPAN :] = one_block[...]
    column = Column(edge_masks()[1])
    for x in range(1, WIDE_X - 2):
        outer = element(
            layer_of(near_one, x, sign), layer_of(far_one, x, sign), *moduli(rows_side, x)
        )
        inner = element(layer_of(near_a, x, sign), layer_of(near_one, x, sign), *moduli(rows, x))
        for c in range(3):
            both = zip(to_lower(outer, c), to_upper(inner, c))
            force_b = column.node((1, c), tuple(one + two for one, two in both))
            force_a = column.node((0, c), to_lower(inner, c))
            if x > 1:
                if c == 0:
                    force_a, force_b = sign * force_a, sign * force_b
                at = ((x - 2) * 3 + c) * SPAN
                block[16:24, at : at + SPAN] = force_a + two_a[(x - 2) * 3 + c]
                at = at + HALF * SPAN
                block[16:24, at : at + SPAN] = force_b
    left = jnp.concatenate(thirds(block[0:16, :]), 0)
    right = jnp.concatenate(thirds(block[8:24, :]), 0)
    products = lax.dot_general(
        left, right, (((1,), (1,)), ((), ())), preferred_element_type=F32
    )
    grams = None
    for one in (2, 1, 0):
        for two in range(2 - one, -1, -1):
            term = products[one * 16 : one * 16 + 16, two * 16 : two * 16 + 16]
            grams = term if grams is None else grams + term
    lanes = lax.broadcasted_iota(jnp.int32, (8, SPAN), 1)
    wide = jnp.concatenate([grams, jnp.zeros((16, SPAN - 16), F32)], 1)
    packed = jnp.where(lanes < 16, pltpu.roll(wide[0:8], 8, 1), pltpu.roll(wide[8:16], 16, 1))
    packed = turned(jnp.where(lanes < 8, norms[...], packed), 1)
    halves = [packed[i : i + 1] + packed[i + 1 : i + 2] for i in (0, 2, 4, 6)]
    packed = jnp.concatenate([halves[0] + halves[1], halves[2] + halves[3]], 0)
    for i in range(message.shape[0]):
        message[i] = packed


def turned(table, way):
    quarter = lax.broadcasted_iota(jnp.int32, (8, SPAN), 0) & 3
    result = table
    for i in range(1, 4):
        result = jnp.where(quarter == i, pltpu.roll(table, (way * 32 * i) % SPAN, 1), result)
    return result


def total_kernel(parts, message):
    total = parts[0]
    for i in range(1, parts.shape[0]):
        total = total + parts[i]
    for i in range(message.shape[0]):
        message[i] = total


def eliminate(table, first):
    rows = lax.broadcasted_iota(jnp.int32, (8, SPAN), 0)
    lanes = lax.broadcasted_iota(jnp.int32, (8, SPAN), 1)
    nothing = jnp.where(lanes < 0, 1.0, 0.0).astype(F32)
    for k in range(0, 8, 2):
        top = jnp.broadcast_to(table[k : k + 1, :], (8, SPAN))
        low = jnp.broadcast_to(table[k + 1 : k + 2, :], (8, SPAN))
        left = jnp.broadcast_to(table[:, first + k : first + k + 1], (8, SPAN)) + nothing
        right = jnp.broadcast_to(table[:, first + k + 1 : first + k + 2], (8, SPAN)) + nothing
        p00 = jnp.broadcast_to(left[k : k + 1, :], (8, SPAN))
        p10 = jnp.broadcast_to(left[k + 1 : k + 2, :], (8, SPAN))
        p01 = jnp.broadcast_to(right[k : k + 1, :], (8, SPAN))
        p11 = jnp.broadcast_to(right[k + 1 : k + 2, :], (8, SPAN))
        scale = 1.0 / (p00 * p11 - p01 * p10)
        new_top = (p11 * top - p01 * low) * scale
        new_low = (p00 * low - p10 * top) * scale
        rest = table - left * new_top - right * new_low
        table = jnp.where(rows == k, new_top, jnp.where(rows == k + 1, new_low, rest))
    return table


def times(left, first, right):
    total = None
    for k in range(8):
        column = jnp.broadcast_to(left[:, first + k : first + k + 1], (8, SPAN))
        row = jnp.broadcast_to(right[k : k + 1, :], (8, SPAN))
        total = column * row if total is None else total + column * row
    return total


def final_kernel(parts, block, solution_rows, residual_rows):
    total = parts[0]
    for i in range(1, parts.shape[0]):
        total = total + parts[i]
    lanes = lax.broadcasted_iota(jnp.int32, (8, SPAN), 1)
    table = jnp.concatenate([jnp.broadcast_to(total[i : i + 1], (4, SPAN)) for i in (0, 1)], 0)
    table = jnp.where(lanes < 32, turned(table, -1), 0.0)
    solved = eliminate(table, 8)
    product = times(table, 16, solved)
    shifted = pltpu.roll(table, SPAN - 8, 1)
    second = jnp.where(lanes < 8, product - shifted, shifted - product)
    coef_c = jnp.where(lanes < 8, eliminate(second, 16), 0.0)
    coef_b = jnp.where(lanes < 8, solved + times(solved, 16, coef_c), 0.0)
    coefs = jnp.concatenate(
        [coef_b, -coef_c - pltpu.roll(coef_b, 8, 1), pltpu.roll(coef_c, 8, 1)], 0
    )[:, 0:16]
    every = block[...]
    mixed = lax.dot_general(
        coefs, every, (((0,), (0,)), ((), ())), precision=HIGHEST, preferred_element_type=F32
    )
    first_core = lax.axis_index("layer_1") == 0
    for half in range(2):
        layer = jnp.where(first_core, 1 - half, half)
        for x in range(OWN_X):
            for c in range(3):
                at = (half * HALF + x * 3 + c) * SPAN
                rows = pl.ds((c * OWN_Z + layer) * OWN_X + x, PROBES, stride=ROWS)
                solution_rows[rows, :] = mixed[0:8, at : at + SPAN]
                residual_rows[rows, :] = every[0:8, at : at + SPAN] + mixed[8:16, at : at + SPAN]


def body(probes, material, lame_pairs):
    tiles = lax.axis_size(TILE)
    in_y = [(i, i ^ 1) for i in range(tiles)]
    in_z = [(i, ((i + 1) ^ 1) - 1) for i in range(1, tiles - 1)]
    in_core = [(0, 1), (1, 0), (2, 3), (3, 2)]
    in_chip = [(1, 2), (2, 1)]
    own, to_y, to_z = call(pack_kernel, (vregs(52), vregs(EDGE), vregs(EDGE)), smem=(0,), outside=(1, 2))(
        lame_pairs.T, probes.reshape(PROBES * ROWS, SPAN), material
    )
    moduli_rows = pltpu.VMEM((64, SPAN), F32)
    shared = (
        vregs(SIDE),
        vregs(SIDE),
        vregs(36),
        vregs(36),
        vregs(FULL),
        vregs(FULL),
        moduli_rows,
    )
    *arrays, edge, norms = call(
        early_kernel,
        (
            *shared,
            vregs(24),
            pltpu.VMEM((8, SPAN), F32),
        ),
    )(own)
    from_z = lax.ppermute(to_z, TILE, in_z)
    from_y = lax.ppermute(to_y, TILE, in_y)
    pairs_a, pairs_b, base_a, base_b, to_a, to_b, rows, probes_block = call(
        inner_kernel,
        (*shared, pltpu.VMEM((8, 2 * HALF * SPAN), F32)),
        aliases={3 + i: i for i in range(7)},
    )(from_y, from_z, edge, *arrays)
    half_block = pltpu.VMEM((8, HALF * SPAN), F32)
    from_b = lax.ppermute(to_b, LAYER, in_chip)
    from_a = lax.ppermute(to_a, LAYER, in_core)
    planes = lax.axis_size(PLANE)
    columns = lax.axis_size(COLUMN)
    scratch = (pltpu.VMEM((SIDE, 8, SPAN), F32), pltpu.VMEM((32, SPAN), F32))
    near_a, one_block_a, two_a = call(
        side_a_kernel,
        (vregs(SIDE), half_block, vregs(HALF)),
        scratch=(*scratch, pltpu.VMEM((SIDE, 8, SPAN), F32)),
    )(from_a, pairs_a, base_a, rows)
    block, message = call(
        side_b_kernel,
        (pltpu.VMEM((24, 2 * HALF * SPAN), F32), pltpu.VMEM((planes, 2, SPAN), F32)),
        scratch=(
            *scratch,
            pltpu.VMEM((SIDE, 8, SPAN), F32),
            pltpu.VMEM((SIDE, 8, SPAN), F32),
            half_block,
        ),
    )(from_b, pairs_b, base_b, rows, near_a, one_block_a, two_a, probes_block, norms)
    parts = lax.all_to_all(message, PLANE, 0, 0, tiled=True)
    message = call(total_kernel, pltpu.VMEM((columns, 2, SPAN), F32))(parts)
    parts = lax.all_to_all(message, COLUMN, 0, 0, tiled=True)
    rows = jax.ShapeDtypeStruct((PROBES * ROWS, SPAN), F32)
    solution_rows, residual_rows = call(final_kernel, (rows, rows))(parts, block)
    return solution_rows.reshape(probes.shape), residual_rows.reshape(probes.shape)


def solution(mesh):
    split = Mesh(
        mesh.devices.reshape(4, 16, 2, 2, 2), ("tile_0", "tile_1", "tile_2", "layer_0", "layer_1")
    )
    spread = P(None, None, LAYER, TILE, None)
    return jax.shard_map(
        body,
        mesh=split,
        in_specs=(spread, P(LAYER, TILE, None), P()),
        out_specs=(spread, spread),
        check_vma=False,
    )
```

```python
import jax
import jax.numpy as jnp
from jax import lax
from jax.experimental import pallas as pl
from jax.experimental.pallas import tpu as pltpu
from jax.sharding import Mesh
from jax.sharding import PartitionSpec as P


TILE = ("tile_0", "tile_1", "tile_2")
LAYER = ("layer_0", "layer_1")
PLANE = ("layer_1", "tile_0", "tile_2", "layer_0")
COLUMN = "tile_1"

PROBES = 8
OWN_Z = 2
OWN_X = 8
WIDE_X = OWN_X + 4
SPAN = 128
ROWS = 3 * OWN_Z * OWN_X
EDGE = 13
FULL = 70
SIDE = 6 * WIDE_X
HALF = 3 * OWN_X
F32 = jnp.float32
HIGHEST = lax.Precision.HIGHEST


def vregs(*shape):
    return pltpu.VMEM((*shape, 8, SPAN), F32)


def call(kernel, out_shape, scratch=(), smem=(), outside=(), aliases=None):
    def run(*args):
        specs = [
            pl.BlockSpec(memory_space=pltpu.SMEM if i in smem else pltpu.VMEM)
            for i in range(len(args))
        ]
        args = [
            arg
            if i in smem or i in outside
            else pltpu.with_memory_space_constraint(arg, pltpu.VMEM)
            for i, arg in enumerate(args)
        ]
        outs = out_shape if isinstance(out_shape, (list, tuple)) else None
        out_specs = (
            [pl.BlockSpec(memory_space=pltpu.VMEM)] * len(outs)
            if outs
            else pl.BlockSpec(memory_space=pltpu.VMEM)
        )
        return pl.pallas_call(
            kernel,
            out_shape=out_shape,
            in_specs=specs,
            out_specs=out_specs,
            scratch_shapes=list(scratch),
            input_output_aliases=aliases or {},
        )(*args)

    return run


def pack_kernel(lame, probes, material, own, to_y, to_z):
    odd = lax.axis_index("tile_2") == 1
    for z in range(OWN_Z):
        for x in range(OWN_X):
            for c in range(3):
                own[(z * OWN_X + x) * 3 + c] = probes[
                    pl.ds((c * OWN_Z + z) * OWN_X + x, PROBES, stride=ROWS), :
                ]
    fields = {}
    for z in range(OWN_Z):
        kinds = material[z]
        for k in range(2):
            value = jnp.where(
                kinds == 0, lame[k, 0], jnp.where(kinds == 1, lame[k, 1], lame[k, 2])
            )
            fields[k, z] = value * (1.0 / 16.0)
            own[48 + k * 2 + z] = fields[k, z]
    first_y = jnp.where(odd, 0, OWN_X - 2)
    first_z = jnp.where(odd, OWN_X - 2, 0)
    for first, to in ((first_y, to_y), (first_z, to_z)):
        for z in range(OWN_Z):
            for xx in range(2):
                for c in range(3):
                    to[(z * 2 + xx) * 3 + c] = own[(z * OWN_X + first + xx) * 3 + c]
    low = jnp.concatenate([fields[k, z][0:2] for k in range(2) for z in range(2)], 0)
    high = jnp.concatenate([fields[k, z][6:8] for k in range(2) for z in range(2)], 0)
    to_y[12] = jnp.where(odd, low, high)
    to_z[12] = jnp.where(odd, high, low)


def stress(modes, lam, mu):
    a, b, e, p, q, r, t = modes
    third = 1.0 / 3.0
    lam3 = lam * third
    mu3 = mu * third
    both = mu + lam3
    top = (4.0 * mu + lam) * (1.0 / 9.0)
    twice = mu + mu
    trace = lam * (a[0] + b[1] + e[2])
    s01 = mu * (b[0] + a[1])
    s02 = mu * (e[0] + a[2])
    s12 = mu * (e[1] + b[2])
    aa = (twice * a[0] + trace, s01, s02)
    bb = (s01, twice * b[1] + trace, s12)
    ee = (s02, s12, twice * e[2] + trace)
    mixed = p[2] + q[1] + r[0]
    pp = (both * p[0] + lam3 * r[2], both * p[1] + lam3 * q[2], mu3 * (p[2] + mixed))
    qq = (both * q[0] + lam3 * r[1], mu3 * (q[1] + mixed), both * q[2] + lam3 * p[1])
    rr = (mu3 * (r[0] + mixed), both * r[1] + lam3 * q[0], both * r[2] + lam3 * p[0])
    tt = tuple(top * t[c] for c in range(3))
    return aa, bb, ee, pp, qq, rr, tt


def along_x(values):
    s0, d0, s1, d1 = values
    return (s0 + s1, s1 - s0, d0 + d1, d1 - d0)


def element(lower, upper, lam, mu):
    modes = tuple(
        tuple(
            upper[c][kind] - lower[c][kind] if minus else upper[c][kind] + lower[c][kind]
            for c in range(3)
        )
        for kind, minus in (
            (0, True),
            (1, False),
            (2, False),
            (1, True),
            (2, True),
            (3, False),
            (3, True),
        )
    )
    return stress(modes, lam, mu)


def to_lower(duals, c):
    aa, bb, ee, pp, qq, rr, tt = duals
    return (-aa[c], bb[c] - pp[c], ee[c] - qq[c], rr[c] - tt[c])


def to_upper(duals, c):
    aa, bb, ee, pp, qq, rr, tt = duals
    return (aa[c], bb[c] + pp[c], ee[c] + qq[c], rr[c] + tt[c])


def edge_masks():
    lanes = lax.broadcasted_iota(jnp.int32, (8, SPAN), 1)
    not_last = jnp.where(lanes == SPAN - 1, 0.0, 1.0).astype(F32)
    not_first = jnp.where(lanes == 0, 0.0, 1.0).astype(F32)
    return not_last, not_first


def spread(value, not_last):
    after = pltpu.roll(value, SPAN - 1, 1) * not_last
    return value + after, after - value


class Column:
    def __init__(self, not_first):
        self.not_first = not_first
        self.left = {}

    def node(self, key, parts):
        ss, ds, sd, dd = parts
        force = self.close(key, ss - ds, sd - dd)
        self.left[key] = (ss + ds, sd + dd)
        return force

    def close(self, key, now_s, now_d):
        if key in self.left:
            now_s = now_s + self.left[key][0]
            now_d = now_d + self.left[key][1]
        return (now_s - now_d) + pltpu.roll(now_s + now_d, 1, 1) * self.not_first


def nodes_of(ref, x, c, sign=None):
    at = (x * 3 + c) * 2
    values = (ref[at], ref[at + 1], ref[at + 6], ref[at + 7])
    if sign is not None and c == 0:
        values = tuple(sign * value for value in values)
    return along_x(values)


def layer_of(ref, x, sign=None):
    return [nodes_of(ref, x, c, sign) for c in range(3)]


def moduli(rows, x):
    return tuple(jnp.broadcast_to(rows[at : at + 1, :], (8, SPAN)) for at in (x, 16 + x))


def pick(first_core, values):
    return (
        jnp.where(first_core, values[1], values[0]),
        jnp.where(first_core, values[0], values[1]),
    )


def early_kernel(
    own, pairs_a, pairs_b, base_a, base_b, to_a, to_b, rows, edge, norms
):
    first_core = lax.axis_index("layer_1") == 0
    sign = jnp.where(first_core, -1.0, 1.0).astype(F32)
    not_last, not_first = edge_masks()
    for x in range(2, 10):
        for c in range(3):
            values = [own[(z * OWN_X + x - 2) * 3 + c] for z in range(OWN_Z)]
            for to, pairs, value in zip(
                (to_a, to_b), (pairs_a, pairs_b), pick(first_core, values)
            ):
                to[x * 3 + c] = value
                pairs[(x * 3 + c) * 2], pairs[(x * 3 + c) * 2 + 1] = spread(value, not_last)
    for z in range(OWN_Z):
        for k in range(2):
            at = (z * 2 + k) * 16
            rows[at : at + 16, :] = jnp.zeros((16, SPAN), F32)
            rows[at + 2 : at + 10, :] = own[48 + k * 2 + z]
    column = Column(not_first)
    for x in range(2, 9):
        duals = element(layer_of(pairs_a, x, sign), layer_of(pairs_b, x, sign), *moduli(rows, x))
        for c in range(3):
            for side, parts in ((0, to_lower(duals, c)), (1, to_upper(duals, c))):
                if x == 2:
                    at = (side * 3 + c) * 2
                    edge[at] = parts[0] - parts[1]
                    edge[at + 1] = parts[2] - parts[3]
                force = column.node((side, c), parts)
                if x > 2:
                    put(side, x, c, sign, force, (base_a, base_b), (to_a, to_b))
    for side in range(2):
        for c in range(3):
            at = 12 + (side * 3 + c) * 2
            edge[at], edge[at + 1] = column.left[side, c]
    for to in (to_a, to_b):
        for x in (0, 1, 10, 11):
            for c in range(3):
                to[x * 3 + c] = jnp.zeros((8, SPAN), F32)
    every = jnp.concatenate([own[i] for i in range(2 * HALF)], 1)
    gram = lax.dot_general(
        every, every, (((1,), (1,)), ((), ())), precision=HIGHEST, preferred_element_type=F32
    )
    norms[...] = jnp.concatenate([gram, jnp.zeros((8, SPAN - 8), F32)], 1)


def put(side, x, c, sign, force, bases, messages):
    force = sign * force if c == 0 else force
    bases[side][x * 3 + c] = force
    messages[side][33 + x * 3 + c] = force


def inner_kernel(
    from_y,
    from_z,
    edge,
    in_pairs_a,
    in_pairs_b,
    in_base_a,
    in_base_b,
    in_to_a,
    in_to_b,
    in_rows,
    pairs_a,
    pairs_b,
    base_a,
    base_b,
    to_a,
    to_b,
    rows,
    probes_block,
):
    odd = lax.axis_index("tile_2") == 1
    first_core = lax.axis_index("layer_1") == 0
    sign = jnp.where(first_core, -1.0, 1.0).astype(F32)
    not_last, not_first = edge_masks()
    for half, source in ((0, in_to_a), (1, in_to_b)):
        for i in range(HALF):
            at = (half * HALF + i) * SPAN
            probes_block[:, at : at + SPAN] = source[6 + i]
    fresh = {}
    for x in (0, 1, 10, 11):
        for c in range(3):
            values = []
            for z in range(OWN_Z):
                at = (z * 2 + x % 10) * 3 + c
                one, two = from_y[at], from_z[at]
                values.append(jnp.where(odd, one, two) if x < 2 else jnp.where(odd, two, one))
            for side, to, pairs, value in zip(
                (0, 1), (to_a, to_b), (pairs_a, pairs_b), pick(first_core, values)
            ):
                to[x * 3 + c] = value
                fresh[side, x, c] = spread(value, not_last)
                at = (x * 3 + c) * 2
                pairs[at], pairs[at + 1] = fresh[side, x, c]
    left = jnp.where(odd, from_y[12], from_z[12])
    right = jnp.where(odd, from_z[12], from_y[12])
    fields = {}
    for z in range(OWN_Z):
        for k in range(2):
            at = (z * 2 + k) * 16
            row = k * 4 + z * 2
            rows[at : at + 2, :] = left[row : row + 2]
            rows[at + 10 : at + 12, :] = right[row : row + 2]
            whole = jnp.concatenate(
                [left[row : row + 2], in_rows[at + 2 : at + 10, :], right[row : row + 2]]
                + [jnp.zeros((4, SPAN), F32)],
                0,
            )
            fields[z, k] = whole
    for k in range(2):
        for i in range(2):
            one, two = pick(first_core, [fields[z, k][i * 8 : i * 8 + 8] for z in range(OWN_Z)])
            to_a[66 + k * 2 + i] = one
            to_b[66 + k * 2 + i] = two

    def layer(side, x):
        source = (in_pairs_a, in_pairs_b)[side]
        combined = []
        for c in range(3):
            values = ()
            for at in (x, x + 1):
                if 2 <= at < 10:
                    values += (source[(at * 3 + c) * 2], source[(at * 3 + c) * 2 + 1])
                else:
                    values += fresh[side, at, c]
            if c == 0:
                values = tuple(sign * value for value in values)
            combined.append(along_x(values))
        return combined

    bases, messages = (base_a, base_b), (to_a, to_b)
    column = Column(not_first)
    for x in (0, 1, 9, 10):
        if x == 9:
            for side in range(2):
                for c in range(3):
                    at = (side * 3 + c) * 2
                    force = column.close((side, c), edge[at], edge[at + 1])
                    put(side, 2, c, sign, force, bases, messages)
                    column.left[side, c] = (edge[12 + at], edge[12 + at + 1])
        lam, mu = (
            jnp.broadcast_to(fields[0, k][x : x + 1], (8, SPAN)) for k in range(2)
        )
        duals = element(layer(0, x), layer(1, x), lam, mu)
        for c in range(3):
            for side, parts in ((0, to_lower(duals, c)), (1, to_upper(duals, c))):
                force = column.node((side, c), parts)
                if x:
                    put(side, x, c, sign, force, bases, messages)


def side_pass(above, other, pairs, base, rows, pairs_other, rows_side, near_one, far_one, one_block, first):
    tile = (lax.axis_index("tile_0") * 16 + lax.axis_index("tile_1")) * 2 + lax.axis_index("tile_2")
    layer = lax.axis_index("layer_0") * 2 + lax.axis_index("layer_1")
    not_last, not_first = edge_masks()
    sign = jnp.where(above, 1.0, -1.0).astype(F32)
    keep_x = jnp.where(tile == 127, 0.0, 1.0).astype(F32)
    keep_z = jnp.where((layer == 3) & above, 0.0, 1.0).astype(F32)
    for x in range(WIDE_X):
        for c in range(3):
            at = (x * 3 + c) * 2
            pairs_other[at], pairs_other[at + 1] = spread(other[x * 3 + c], not_last)
    for i in range(4):
        rows_side[i * 8 : i * 8 + 8, :] = jnp.where(
            above, rows[32 + i * 8 : 40 + i * 8, :], other[66 + i]
        )
    column = Column(not_first)
    for x in range(WIDE_X - 1):
        duals = element(
            layer_of(pairs, x, sign), layer_of(pairs_other, x, sign), *moduli(rows_side, x)
        )
        for c in range(3):
            near = column.node((0, c), to_lower(duals, c))
            far = column.node((1, c), to_upper(duals, c))
            if x:
                if c == 0:
                    near, far = sign * near, sign * far
                near = near + base[x * 3 + c]
                far = (far + other[33 + x * 3 + c]) * keep_z
                if x == 10:
                    near, far = near * keep_x, far * keep_x
                if 2 <= x < 10:
                    at = (first + (x - 2) * 3 + c) * SPAN
                    one_block[:, at : at + SPAN] = near
                at = (x * 3 + c) * 2
                near_one[at], near_one[at + 1] = spread(near, not_last)
                far_one[at], far_one[at + 1] = spread(far, not_last)
    return sign


def thirds(values):
    high = values.astype(jnp.bfloat16)
    rest = values - high.astype(F32)
    middle = rest.astype(jnp.bfloat16)
    low = (rest - middle.astype(F32)).astype(jnp.bfloat16)
    return high, middle, low


def side_a_kernel(
    other, pairs, base, rows, near_one, one_block, two_side, pairs_other, rows_side, far_one
):
    above = lax.axis_index("layer_1") == 0
    sign = side_pass(
        above, other, pairs, base, rows, pairs_other, rows_side, near_one, far_one, one_block, 0
    )
    column = Column(edge_masks()[1])
    for x in range(1, WIDE_X - 2):
        duals = element(
            layer_of(near_one, x, sign), layer_of(far_one, x, sign), *moduli(rows_side, x)
        )
        for c in range(3):
            force = column.node(c, to_lower(duals, c))
            if x > 1:
                two_side[(x - 2) * 3 + c] = sign * force if c == 0 else force


def side_b_kernel(
    other,
    pairs,
    base,
    rows,
    near_a,
    one_block_a,
    two_a,
    probes_block,
    norms,
    block,
    message,
    pairs_other,
    rows_side,
    near_one,
    far_one,
    one_block,
):
    above = lax.axis_index("layer_1") == 1
    block[0:8, :] = probes_block[...]
    block[8:16, 0 : HALF * SPAN] = one_block_a[...]
    sign = side_pass(
        above, other, pairs, base, rows, pairs_other, rows_side, near_one, far_one, one_block, 0
    )
    block[8:16, HALF * SPAN :] = one_block[...]
    column = Column(edge_masks()[1])
    for x in range(1, WIDE_X - 2):
        outer = element(
            layer_of(near_one, x, sign), layer_of(far_one, x, sign), *moduli(rows_side, x)
        )
        inner = element(layer_of(near_a, x, sign), layer_of(near_one, x, sign), *moduli(rows, x))
        for c in range(3):
            both = zip(to_lower(outer, c), to_upper(inner, c))
            force_b = column.node((1, c), tuple(one + two for one, two in both))
            force_a = column.node((0, c), to_lower(inner, c))
            if x > 1:
                if c == 0:
                    force_a, force_b = sign * force_a, sign * force_b
                at = ((x - 2) * 3 + c) * SPAN
                block[16:24, at : at + SPAN] = force_a + two_a[(x - 2) * 3 + c]
                at = at + HALF * SPAN
                block[16:24, at : at + SPAN] = force_b
    left = jnp.concatenate(thirds(block[0:16, :]), 0)
    right = jnp.concatenate(thirds(block[8:24, :]), 0)
    products = lax.dot_general(
        left, right, (((1,), (1,)), ((), ())), preferred_element_type=F32
    )
    grams = None
    for one in (2, 1, 0):
        for two in range(2 - one, -1, -1):
            term = products[one * 16 : one * 16 + 16, two * 16 : two * 16 + 16]
            grams = term if grams is None else grams + term
    lanes = lax.broadcasted_iota(jnp.int32, (8, SPAN), 1)
    wide = jnp.concatenate([grams, jnp.zeros((16, SPAN - 16), F32)], 1)
    packed = jnp.where(lanes < 16, pltpu.roll(wide[0:8], 8, 1), pltpu.roll(wide[8:16], 16, 1))
    packed = turned(jnp.where(lanes < 8, norms[...], packed), 1)
    halves = [packed[i : i + 1] + packed[i + 1 : i + 2] for i in (0, 2, 4, 6)]
    packed = jnp.concatenate([halves[0] + halves[1], halves[2] + halves[3]], 0)
    for i in range(message.shape[0]):
        message[i] = packed


def turned(table, way):
    quarter = lax.broadcasted_iota(jnp.int32, (8, SPAN), 0) & 3
    result = table
    for i in range(1, 4):
        result = jnp.where(quarter == i, pltpu.roll(table, (way * 32 * i) % SPAN, 1), result)
    return result


def total_kernel(parts, message):
    total = parts[0]
    for i in range(1, parts.shape[0]):
        total = total + parts[i]
    for i in range(message.shape[0]):
        message[i] = total


def eliminate(table, first):
    rows = lax.broadcasted_iota(jnp.int32, (8, SPAN), 0)
    lanes = lax.broadcasted_iota(jnp.int32, (8, SPAN), 1)
    nothing = jnp.where(lanes < 0, 1.0, 0.0).astype(F32)
    for k in range(0, 8, 2):
        top = jnp.broadcast_to(table[k : k + 1, :], (8, SPAN))
        low = jnp.broadcast_to(table[k + 1 : k + 2, :], (8, SPAN))
        left = jnp.broadcast_to(table[:, first + k : first + k + 1], (8, SPAN)) + nothing
        right = jnp.broadcast_to(table[:, first + k + 1 : first + k + 2], (8, SPAN)) + nothing
        p00 = jnp.broadcast_to(left[k : k + 1, :], (8, SPAN))
        p10 = jnp.broadcast_to(left[k + 1 : k + 2, :], (8, SPAN))
        p01 = jnp.broadcast_to(right[k : k + 1, :], (8, SPAN))
        p11 = jnp.broadcast_to(right[k + 1 : k + 2, :], (8, SPAN))
        scale = 1.0 / (p00 * p11 - p01 * p10)
        new_top = (p11 * top - p01 * low) * scale
        new_low = (p00 * low - p10 * top) * scale
        rest = table - left * new_top - right * new_low
        table = jnp.where(rows == k, new_top, jnp.where(rows == k + 1, new_low, rest))
    return table


def times(left, first, right):
    total = None
    for k in range(8):
        column = jnp.broadcast_to(left[:, first + k : first + k + 1], (8, SPAN))
        row = jnp.broadcast_to(right[k : k + 1, :], (8, SPAN))
        total = column * row if total is None else total + column * row
    return total


def final_kernel(parts, block, solution_rows, residual_rows):
    total = parts[0]
    for i in range(1, parts.shape[0]):
        total = total + parts[i]
    lanes = lax.broadcasted_iota(jnp.int32, (8, SPAN), 1)
    table = jnp.concatenate([jnp.broadcast_to(total[i : i + 1], (4, SPAN)) for i in (0, 1)], 0)
    table = jnp.where(lanes < 32, turned(table, -1), 0.0)
    solved = eliminate(table, 8)
    product = times(table, 16, solved)
    shifted = pltpu.roll(table, SPAN - 8, 1)
    second = jnp.where(lanes < 8, product - shifted, shifted - product)
    coef_c = jnp.where(lanes < 8, eliminate(second, 16), 0.0)
    coef_b = jnp.where(lanes < 8, solved + times(solved, 16, coef_c), 0.0)
    coefs = jnp.concatenate(
        [coef_b, -coef_c - pltpu.roll(coef_b, 8, 1), pltpu.roll(coef_c, 8, 1)], 0
    )[:, 0:16]
    every = block[...]
    ones, twos = (
        jnp.concatenate([parts_of[i].astype(F32) for i in order], 0).astype(jnp.bfloat16)
        for parts_of, order in (
            (thirds(coefs), (2, 1, 0, 1, 0, 0)),
            (thirds(every), (0, 1, 2, 0, 1, 0)),
        )
    )
    mixed = lax.dot_general(
        ones, twos, (((0,), (0,)), ((), ())), preferred_element_type=F32
    )
    first_core = lax.axis_index("layer_1") == 0
    for half in range(2):
        layer = jnp.where(first_core, 1 - half, half)
        for x in range(OWN_X):
            for c in range(3):
                at = (half * HALF + x * 3 + c) * SPAN
                rows = pl.ds((c * OWN_Z + layer) * OWN_X + x, PROBES, stride=ROWS)
                solution_rows[rows, :] = mixed[0:8, at : at + SPAN]
                residual_rows[rows, :] = every[0:8, at : at + SPAN] + mixed[8:16, at : at + SPAN]


def body(probes, material, lame_pairs):
    tiles = lax.axis_size(TILE)
    in_y = [(i, i ^ 1) for i in range(tiles)]
    in_z = [(i, ((i + 1) ^ 1) - 1) for i in range(1, tiles - 1)]
    in_core = [(0, 1), (1, 0), (2, 3), (3, 2)]
    in_chip = [(1, 2), (2, 1)]
    own, to_y, to_z = call(pack_kernel, (vregs(52), vregs(EDGE), vregs(EDGE)), smem=(0,), outside=(1, 2))(
        lame_pairs.T, probes.reshape(PROBES * ROWS, SPAN), material
    )
    moduli_rows = pltpu.VMEM((64, SPAN), F32)
    shared = (
        vregs(SIDE),
        vregs(SIDE),
        vregs(36),
        vregs(36),
        vregs(FULL),
        vregs(FULL),
        moduli_rows,
    )
    *arrays, edge, norms = call(
        early_kernel,
        (
            *shared,
            vregs(24),
            pltpu.VMEM((8, SPAN), F32),
        ),
    )(own)
    from_z = lax.ppermute(to_z, TILE, in_z)
    from_y = lax.ppermute(to_y, TILE, in_y)
    pairs_a, pairs_b, base_a, base_b, to_a, to_b, rows, probes_block = call(
        inner_kernel,
        (*shared, pltpu.VMEM((8, 2 * HALF * SPAN), F32)),
        aliases={3 + i: i for i in range(7)},
    )(from_y, from_z, edge, *arrays)
    half_block = pltpu.VMEM((8, HALF * SPAN), F32)
    from_b = lax.ppermute(to_b, LAYER, in_chip)
    from_a = lax.ppermute(to_a, LAYER, in_core)
    planes = lax.axis_size(PLANE)
    columns = lax.axis_size(COLUMN)
    scratch = (pltpu.VMEM((SIDE, 8, SPAN), F32), pltpu.VMEM((32, SPAN), F32))
    near_a, one_block_a, two_a = call(
        side_a_kernel,
        (vregs(SIDE), half_block, vregs(HALF)),
        scratch=(*scratch, pltpu.VMEM((SIDE, 8, SPAN), F32)),
    )(from_a, pairs_a, base_a, rows)
    block, message = call(
        side_b_kernel,
        (pltpu.VMEM((24, 2 * HALF * SPAN), F32), pltpu.VMEM((planes, 2, SPAN), F32)),
        scratch=(
            *scratch,
            pltpu.VMEM((SIDE, 8, SPAN), F32),
            pltpu.VMEM((SIDE, 8, SPAN), F32),
            half_block,
        ),
    )(from_b, pairs_b, base_b, rows, near_a, one_block_a, two_a, probes_block, norms)
    parts = lax.all_to_all(message, PLANE, 0, 0, tiled=True)
    message = call(total_kernel, pltpu.VMEM((columns, 2, SPAN), F32))(parts)
    parts = lax.all_to_all(message, COLUMN, 0, 0, tiled=True)
    rows = jax.ShapeDtypeStruct((PROBES * ROWS, SPAN), F32)
    solution_rows, residual_rows = call(final_kernel, (rows, rows))(parts, block)
    return solution_rows.reshape(probes.shape), residual_rows.reshape(probes.shape)


def solution(mesh):
    split = Mesh(
        mesh.devices.reshape(4, 16, 2, 2, 2), ("tile_0", "tile_1", "tile_2", "layer_0", "layer_1")
    )
    spread = P(None, None, LAYER, TILE, None)
    return jax.shard_map(
        body,
        mesh=split,
        in_specs=(spread, P(LAYER, TILE, None), P()),
        out_specs=(spread, spread),
        check_vma=False,
    )
```

```python
import jax
import jax.numpy as jnp
from jax import lax
from jax.experimental import pallas as pl
from jax.experimental.pallas import tpu as pltpu
from jax.sharding import Mesh
from jax.sharding import PartitionSpec as P


TILE = ("tile_0", "tile_1", "tile_2")
LAYER = ("layer_0", "layer_1")
PLANE = ("layer_1", "tile_0", "tile_2", "layer_0")
COLUMN = "tile_1"

PROBES = 8
OWN_Z = 2
OWN_X = 8
WIDE_X = OWN_X + 4
SPAN = 128
ROWS = 3 * OWN_Z * OWN_X
EDGE = 13
FULL = 70
SIDE = 6 * WIDE_X
HALF = 3 * OWN_X
F32 = jnp.float32
HIGHEST = lax.Precision.HIGHEST


def vregs(*shape):
    return pltpu.VMEM((*shape, 8, SPAN), F32)


def call(kernel, out_shape, scratch=(), smem=(), outside=(), aliases=None):
    def run(*args):
        specs = [
            pl.BlockSpec(memory_space=pltpu.SMEM if i in smem else pltpu.VMEM)
            for i in range(len(args))
        ]
        args = [
            arg
            if i in smem or i in outside
            else pltpu.with_memory_space_constraint(arg, pltpu.VMEM)
            for i, arg in enumerate(args)
        ]
        outs = out_shape if isinstance(out_shape, (list, tuple)) else None
        out_specs = (
            [pl.BlockSpec(memory_space=pltpu.VMEM)] * len(outs)
            if outs
            else pl.BlockSpec(memory_space=pltpu.VMEM)
        )
        return pl.pallas_call(
            kernel,
            out_shape=out_shape,
            in_specs=specs,
            out_specs=out_specs,
            scratch_shapes=list(scratch),
            input_output_aliases=aliases or {},
        )(*args)

    return run


def pack_kernel(lame, probes, material, own, to_y, to_z):
    odd = lax.axis_index("tile_2") == 1
    for z in range(OWN_Z):
        for x in range(OWN_X):
            for c in range(3):
                own[(z * OWN_X + x) * 3 + c] = probes[
                    pl.ds((c * OWN_Z + z) * OWN_X + x, PROBES, stride=ROWS), :
                ]
    fields = {}
    for z in range(OWN_Z):
        kinds = material[z]
        for k in range(2):
            value = jnp.where(
                kinds == 0, lame[k, 0], jnp.where(kinds == 1, lame[k, 1], lame[k, 2])
            )
            fields[k, z] = value * (1.0 / 16.0)
            own[48 + k * 2 + z] = fields[k, z]
    first_y = jnp.where(odd, 0, OWN_X - 2)
    first_z = jnp.where(odd, OWN_X - 2, 0)
    for first, to in ((first_y, to_y), (first_z, to_z)):
        for z in range(OWN_Z):
            for xx in range(2):
                for c in range(3):
                    to[(z * 2 + xx) * 3 + c] = own[(z * OWN_X + first + xx) * 3 + c]
    low = jnp.concatenate([fields[k, z][0:2] for k in range(2) for z in range(2)], 0)
    high = jnp.concatenate([fields[k, z][6:8] for k in range(2) for z in range(2)], 0)
    to_y[12] = jnp.where(odd, low, high)
    to_z[12] = jnp.where(odd, high, low)


def stress(modes, lam, mu):
    a, b, e, p, q, r, t = modes
    third = 1.0 / 3.0
    lam3 = lam * third
    mu3 = mu * third
    both = mu + lam3
    top = (4.0 * mu + lam) * (1.0 / 9.0)
    twice = mu + mu
    trace = lam * (a[0] + b[1] + e[2])
    s01 = mu * (b[0] + a[1])
    s02 = mu * (e[0] + a[2])
    s12 = mu * (e[1] + b[2])
    aa = (twice * a[0] + trace, s01, s02)
    bb = (s01, twice * b[1] + trace, s12)
    ee = (s02, s12, twice * e[2] + trace)
    mixed = p[2] + q[1] + r[0]
    pp = (both * p[0] + lam3 * r[2], both * p[1] + lam3 * q[2], mu3 * (p[2] + mixed))
    qq = (both * q[0] + lam3 * r[1], mu3 * (q[1] + mixed), both * q[2] + lam3 * p[1])
    rr = (mu3 * (r[0] + mixed), both * r[1] + lam3 * q[0], both * r[2] + lam3 * p[0])
    tt = tuple(top * t[c] for c in range(3))
    return aa, bb, ee, pp, qq, rr, tt


def along_x(values):
    s0, d0, s1, d1 = values
    return (s0 + s1, s1 - s0, d0 + d1, d1 - d0)


def element(lower, upper, lam, mu):
    modes = tuple(
        tuple(
            upper[c][kind] - lower[c][kind] if minus else upper[c][kind] + lower[c][kind]
            for c in range(3)
        )
        for kind, minus in (
            (0, True),
            (1, False),
            (2, False),
            (1, True),
            (2, True),
            (3, False),
            (3, True),
        )
    )
    return stress(modes, lam, mu)


def to_lower(duals, c):
    aa, bb, ee, pp, qq, rr, tt = duals
    return (-aa[c], bb[c] - pp[c], ee[c] - qq[c], rr[c] - tt[c])


def to_upper(duals, c):
    aa, bb, ee, pp, qq, rr, tt = duals
    return (aa[c], bb[c] + pp[c], ee[c] + qq[c], rr[c] + tt[c])


def edge_masks():
    lanes = lax.broadcasted_iota(jnp.int32, (8, SPAN), 1)
    not_last = jnp.where(lanes == SPAN - 1, 0.0, 1.0).astype(F32)
    not_first = jnp.where(lanes == 0, 0.0, 1.0).astype(F32)
    return not_last, not_first


def spread(value, not_last):
    after = pltpu.roll(value, SPAN - 1, 1) * not_last
    return value + after, after - value


class Column:
    def __init__(self, not_first):
        self.not_first = not_first
        self.left = {}

    def node(self, key, parts):
        ss, ds, sd, dd = parts
        force = self.close(key, ss - ds, sd - dd)
        self.left[key] = (ss + ds, sd + dd)
        return force

    def close(self, key, now_s, now_d):
        if key in self.left:
            now_s = now_s + self.left[key][0]
            now_d = now_d + self.left[key][1]
        return (now_s - now_d) + pltpu.roll(now_s + now_d, 1, 1) * self.not_first


def nodes_of(ref, x, c, sign=None):
    at = (x * 3 + c) * 2
    values = (ref[at], ref[at + 1], ref[at + 6], ref[at + 7])
    if sign is not None and c == 0:
        values = tuple(sign * value for value in values)
    return along_x(values)


def layer_of(ref, x, sign=None):
    return [nodes_of(ref, x, c, sign) for c in range(3)]


def moduli(rows, x):
    return tuple(jnp.broadcast_to(rows[at : at + 1, :], (8, SPAN)) for at in (x, 16 + x))


def pick(first_core, values):
    return (
        jnp.where(first_core, values[1], values[0]),
        jnp.where(first_core, values[0], values[1]),
    )


def early_kernel(
    own, pairs_a, pairs_b, base_a, base_b, to_a, to_b, rows, edge, norms
):
    first_core = lax.axis_index("layer_1") == 0
    sign = jnp.where(first_core, -1.0, 1.0).astype(F32)
    not_last, not_first = edge_masks()
    for x in range(2, 10):
        for c in range(3):
            values = [own[(z * OWN_X + x - 2) * 3 + c] for z in range(OWN_Z)]
            for to, pairs, value in zip(
                (to_a, to_b), (pairs_a, pairs_b), pick(first_core, values)
            ):
                to[x * 3 + c] = value
                pairs[(x * 3 + c) * 2], pairs[(x * 3 + c) * 2 + 1] = spread(value, not_last)
    for z in range(OWN_Z):
        for k in range(2):
            at = (z * 2 + k) * 16
            rows[at : at + 16, :] = jnp.zeros((16, SPAN), F32)
            rows[at + 2 : at + 10, :] = own[48 + k * 2 + z]
    column = Column(not_first)
    for x in range(2, 9):
        duals = element(layer_of(pairs_a, x, sign), layer_of(pairs_b, x, sign), *moduli(rows, x))
        for c in range(3):
            for side, parts in ((0, to_lower(duals, c)), (1, to_upper(duals, c))):
                if x == 2:
                    at = (side * 3 + c) * 2
                    edge[at] = parts[0] - parts[1]
                    edge[at + 1] = parts[2] - parts[3]
                force = column.node((side, c), parts)
                if x > 2:
                    put(side, x, c, sign, force, (base_a, base_b), (to_a, to_b))
    for side in range(2):
        for c in range(3):
            at = 12 + (side * 3 + c) * 2
            edge[at], edge[at + 1] = column.left[side, c]
    for to in (to_a, to_b):
        for x in (0, 1, 10, 11):
            for c in range(3):
                to[x * 3 + c] = jnp.zeros((8, SPAN), F32)
    every = jnp.concatenate([own[i] for i in range(2 * HALF)], 1)
    gram = lax.dot_general(
        every, every, (((1,), (1,)), ((), ())), precision=HIGHEST, preferred_element_type=F32
    )
    norms[...] = jnp.concatenate([gram, jnp.zeros((8, SPAN - 8), F32)], 1)


def put(side, x, c, sign, force, bases, messages):
    force = sign * force if c == 0 else force
    bases[side][x * 3 + c] = force
    messages[side][33 + x * 3 + c] = force


def inner_kernel(
    from_y,
    from_z,
    edge,
    in_pairs_a,
    in_pairs_b,
    in_base_a,
    in_base_b,
    in_to_a,
    in_to_b,
    in_rows,
    pairs_a,
    pairs_b,
    base_a,
    base_b,
    to_a,
    to_b,
    rows,
    probes_block,
):
    odd = lax.axis_index("tile_2") == 1
    first_core = lax.axis_index("layer_1") == 0
    sign = jnp.where(first_core, -1.0, 1.0).astype(F32)
    not_last, not_first = edge_masks()
    for half, source in ((0, in_to_a), (1, in_to_b)):
        for i in range(HALF):
            at = (half * HALF + i) * SPAN
            probes_block[:, at : at + SPAN] = source[6 + i]
    fresh = {}
    for x in (0, 1, 10, 11):
        for c in range(3):
            values = []
            for z in range(OWN_Z):
                at = (z * 2 + x % 10) * 3 + c
                one, two = from_y[at], from_z[at]
                values.append(jnp.where(odd, one, two) if x < 2 else jnp.where(odd, two, one))
            for side, to, pairs, value in zip(
                (0, 1), (to_a, to_b), (pairs_a, pairs_b), pick(first_core, values)
            ):
                to[x * 3 + c] = value
                fresh[side, x, c] = spread(value, not_last)
                at = (x * 3 + c) * 2
                pairs[at], pairs[at + 1] = fresh[side, x, c]
    left = jnp.where(odd, from_y[12], from_z[12])
    right = jnp.where(odd, from_z[12], from_y[12])
    fields = {}
    for z in range(OWN_Z):
        for k in range(2):
            at = (z * 2 + k) * 16
            row = k * 4 + z * 2
            rows[at : at + 2, :] = left[row : row + 2]
            rows[at + 10 : at + 12, :] = right[row : row + 2]
            whole = jnp.concatenate(
                [left[row : row + 2], in_rows[at + 2 : at + 10, :], right[row : row + 2]]
                + [jnp.zeros((4, SPAN), F32)],
                0,
            )
            fields[z, k] = whole
    for k in range(2):
        for i in range(2):
            one, two = pick(first_core, [fields[z, k][i * 8 : i * 8 + 8] for z in range(OWN_Z)])
            to_a[66 + k * 2 + i] = one
            to_b[66 + k * 2 + i] = two

    def layer(side, x):
        source = (in_pairs_a, in_pairs_b)[side]
        combined = []
        for c in range(3):
            values = ()
            for at in (x, x + 1):
                if 2 <= at < 10:
                    values += (source[(at * 3 + c) * 2], source[(at * 3 + c) * 2 + 1])
                else:
                    values += fresh[side, at, c]
            if c == 0:
                values = tuple(sign * value for value in values)
            combined.append(along_x(values))
        return combined

    bases, messages = (base_a, base_b), (to_a, to_b)
    column = Column(not_first)
    for x in (0, 1, 9, 10):
        if x == 9:
            for side in range(2):
                for c in range(3):
                    at = (side * 3 + c) * 2
                    force = column.close((side, c), edge[at], edge[at + 1])
                    put(side, 2, c, sign, force, bases, messages)
                    column.left[side, c] = (edge[12 + at], edge[12 + at + 1])
        lam, mu = (
            jnp.broadcast_to(fields[0, k][x : x + 1], (8, SPAN)) for k in range(2)
        )
        duals = element(layer(0, x), layer(1, x), lam, mu)
        for c in range(3):
            for side, parts in ((0, to_lower(duals, c)), (1, to_upper(duals, c))):
                force = column.node((side, c), parts)
                if x:
                    put(side, x, c, sign, force, bases, messages)


def side_pass(above, other, pairs, base, rows, pairs_other, rows_side, near_one, far_one, one_block, first):
    tile = (lax.axis_index("tile_0") * 16 + lax.axis_index("tile_1")) * 2 + lax.axis_index("tile_2")
    layer = lax.axis_index("layer_0") * 2 + lax.axis_index("layer_1")
    not_last, not_first = edge_masks()
    sign = jnp.where(above, 1.0, -1.0).astype(F32)
    keep_x = jnp.where(tile == 127, 0.0, 1.0).astype(F32)
    keep_z = jnp.where((layer == 3) & above, 0.0, 1.0).astype(F32)
    for x in range(WIDE_X):
        for c in range(3):
            at = (x * 3 + c) * 2
            pairs_other[at], pairs_other[at + 1] = spread(other[x * 3 + c], not_last)
    for i in range(4):
        rows_side[i * 8 : i * 8 + 8, :] = jnp.where(
            above, rows[32 + i * 8 : 40 + i * 8, :], other[66 + i]
        )
    column = Column(not_first)
    for x in range(WIDE_X - 1):
        duals = element(
            layer_of(pairs, x, sign), layer_of(pairs_other, x, sign), *moduli(rows_side, x)
        )
        for c in range(3):
            near = column.node((0, c), to_lower(duals, c))
            far = column.node((1, c), to_upper(duals, c))
            if x:
                if c == 0:
                    near, far = sign * near, sign * far
                near = near + base[x * 3 + c]
                far = (far + other[33 + x * 3 + c]) * keep_z
                if x == 10:
                    near, far = near * keep_x, far * keep_x
                if 2 <= x < 10:
                    at = (first + (x - 2) * 3 + c) * SPAN
                    one_block[:, at : at + SPAN] = near
                at = (x * 3 + c) * 2
                near_one[at], near_one[at + 1] = spread(near, not_last)
                far_one[at], far_one[at + 1] = spread(far, not_last)
    return sign


def thirds(values):
    high = values.astype(jnp.bfloat16)
    rest = values - high.astype(F32)
    middle = rest.astype(jnp.bfloat16)
    low = (rest - middle.astype(F32)).astype(jnp.bfloat16)
    return high, middle, low


def side_a_kernel(
    other, pairs, base, rows, near_one, one_block, two_side, pairs_other, rows_side, far_one
):
    above = lax.axis_index("layer_1") == 0
    sign = side_pass(
        above, other, pairs, base, rows, pairs_other, rows_side, near_one, far_one, one_block, 0
    )
    column = Column(edge_masks()[1])
    for x in range(1, WIDE_X - 2):
        duals = element(
            layer_of(near_one, x, sign), layer_of(far_one, x, sign), *moduli(rows_side, x)
        )
        for c in range(3):
            force = column.node(c, to_lower(duals, c))
            if x > 1:
                two_side[(x - 2) * 3 + c] = sign * force if c == 0 else force


def side_b_kernel(
    other,
    pairs,
    base,
    rows,
    near_a,
    one_block_a,
    two_a,
    probes_block,
    norms,
    block,
    message,
    pairs_other,
    rows_side,
    near_one,
    far_one,
    one_block,
):
    above = lax.axis_index("layer_1") == 1
    block[0:8, :] = probes_block[...]
    block[8:16, 0 : HALF * SPAN] = one_block_a[...]
    sign = side_pass(
        above, other, pairs, base, rows, pairs_other, rows_side, near_one, far_one, one_block, 0
    )
    block[8:16, HALF * SPAN :] = one_block[...]
    column = Column(edge_masks()[1])
    for x in range(1, WIDE_X - 2):
        outer = element(
            layer_of(near_one, x, sign), layer_of(far_one, x, sign), *moduli(rows_side, x)
        )
        inner = element(layer_of(near_a, x, sign), layer_of(near_one, x, sign), *moduli(rows, x))
        for c in range(3):
            both = zip(to_lower(outer, c), to_upper(inner, c))
            force_b = column.node((1, c), tuple(one + two for one, two in both))
            force_a = column.node((0, c), to_lower(inner, c))
            if x > 1:
                if c == 0:
                    force_a, force_b = sign * force_a, sign * force_b
                at = ((x - 2) * 3 + c) * SPAN
                block[16:24, at : at + SPAN] = force_a + two_a[(x - 2) * 3 + c]
                at = at + HALF * SPAN
                block[16:24, at : at + SPAN] = force_b
    split = [part.astype(F32) for part in thirds(block[...])]
    left = jnp.concatenate([part[0:16] for part in split], 0).astype(jnp.bfloat16)
    right = jnp.concatenate([part[8:24] for part in split], 0).astype(jnp.bfloat16)
    products = lax.dot_general(
        left, right, (((1,), (1,)), ((), ())), preferred_element_type=F32
    )
    grams = None
    for one in (2, 1, 0):
        for two in range(2 - one, -1, -1):
            term = products[one * 16 : one * 16 + 16, two * 16 : two * 16 + 16]
            grams = term if grams is None else grams + term
    lanes = lax.broadcasted_iota(jnp.int32, (8, SPAN), 1)
    wide = jnp.concatenate([grams, jnp.zeros((16, SPAN - 16), F32)], 1)
    packed = jnp.where(lanes < 16, pltpu.roll(wide[0:8], 8, 1), pltpu.roll(wide[8:16], 16, 1))
    packed = turned(jnp.where(lanes < 8, norms[...], packed), 1)
    halves = [packed[i : i + 1] + packed[i + 1 : i + 2] for i in (0, 2, 4, 6)]
    packed = jnp.concatenate([halves[0] + halves[1], halves[2] + halves[3]], 0)
    for i in range(message.shape[0]):
        message[i] = packed


def turned(table, way):
    quarter = lax.broadcasted_iota(jnp.int32, (8, SPAN), 0) & 3
    result = table
    for i in range(1, 4):
        result = jnp.where(quarter == i, pltpu.roll(table, (way * 32 * i) % SPAN, 1), result)
    return result


def total_kernel(parts, message):
    total = parts[0]
    for i in range(1, parts.shape[0]):
        total = total + parts[i]
    for i in range(message.shape[0]):
        message[i] = total


def eliminate(table, first):
    rows = lax.broadcasted_iota(jnp.int32, (8, SPAN), 0)
    lanes = lax.broadcasted_iota(jnp.int32, (8, SPAN), 1)
    nothing = jnp.where(lanes < 0, 1.0, 0.0).astype(F32)
    for k in range(0, 8, 2):
        top = jnp.broadcast_to(table[k : k + 1, :], (8, SPAN))
        low = jnp.broadcast_to(table[k + 1 : k + 2, :], (8, SPAN))
        left = jnp.broadcast_to(table[:, first + k : first + k + 1], (8, SPAN)) + nothing
        right = jnp.broadcast_to(table[:, first + k + 1 : first + k + 2], (8, SPAN)) + nothing
        p00 = jnp.broadcast_to(left[k : k + 1, :], (8, SPAN))
        p10 = jnp.broadcast_to(left[k + 1 : k + 2, :], (8, SPAN))
        p01 = jnp.broadcast_to(right[k : k + 1, :], (8, SPAN))
        p11 = jnp.broadcast_to(right[k + 1 : k + 2, :], (8, SPAN))
        scale = 1.0 / (p00 * p11 - p01 * p10)
        new_top = (p11 * top - p01 * low) * scale
        new_low = (p00 * low - p10 * top) * scale
        rest = table - left * new_top - right * new_low
        table = jnp.where(rows == k, new_top, jnp.where(rows == k + 1, new_low, rest))
    return table


def times(left, first, right):
    total = None
    for k in range(8):
        column = jnp.broadcast_to(left[:, first + k : first + k + 1], (8, SPAN))
        row = jnp.broadcast_to(right[k : k + 1, :], (8, SPAN))
        total = column * row if total is None else total + column * row
    return total


def final_kernel(parts, block, solution_rows, residual_rows):
    total = parts[0]
    for i in range(1, parts.shape[0]):
        total = total + parts[i]
    lanes = lax.broadcasted_iota(jnp.int32, (8, SPAN), 1)
    table = jnp.concatenate([jnp.broadcast_to(total[i : i + 1], (4, SPAN)) for i in (0, 1)], 0)
    table = jnp.where(lanes < 32, turned(table, -1), 0.0)
    solved = eliminate(table, 8)
    product = times(table, 16, solved)
    shifted = pltpu.roll(table, SPAN - 8, 1)
    second = jnp.where(lanes < 8, product - shifted, shifted - product)
    coef_c = jnp.where(lanes < 8, eliminate(second, 16), 0.0)
    coef_b = jnp.where(lanes < 8, solved + times(solved, 16, coef_c), 0.0)
    coefs = jnp.concatenate(
        [coef_b, -coef_c - pltpu.roll(coef_b, 8, 1), pltpu.roll(coef_c, 8, 1)], 0
    )[:, 0:16]
    every = block[...]
    ones, twos = (
        jnp.concatenate([parts_of[i].astype(F32) for i in order], 0).astype(jnp.bfloat16)
        for parts_of, order in (
            (thirds(coefs), (2, 1, 0, 1, 0, 0)),
            (thirds(every), (0, 1, 2, 0, 1, 0)),
        )
    )
    mixed = lax.dot_general(
        ones, twos, (((0,), (0,)), ((), ())), preferred_element_type=F32
    )
    first_core = lax.axis_index("layer_1") == 0
    for half in range(2):
        layer = jnp.where(first_core, 1 - half, half)
        for x in range(OWN_X):
            for c in range(3):
                at = (half * HALF + x * 3 + c) * SPAN
                rows = pl.ds((c * OWN_Z + layer) * OWN_X + x, PROBES, stride=ROWS)
                solution_rows[rows, :] = mixed[0:8, at : at + SPAN]
                residual_rows[rows, :] = every[0:8, at : at + SPAN] + mixed[8:16, at : at + SPAN]


def body(probes, material, lame_pairs):
    tiles = lax.axis_size(TILE)
    in_y = [(i, i ^ 1) for i in range(tiles)]
    in_z = [(i, ((i + 1) ^ 1) - 1) for i in range(1, tiles - 1)]
    in_core = [(0, 1), (1, 0), (2, 3), (3, 2)]
    in_chip = [(1, 2), (2, 1)]
    own, to_y, to_z = call(pack_kernel, (vregs(52), vregs(EDGE), vregs(EDGE)), smem=(0,), outside=(1, 2))(
        lame_pairs.T, probes.reshape(PROBES * ROWS, SPAN), material
    )
    moduli_rows = pltpu.VMEM((64, SPAN), F32)
    shared = (
        vregs(SIDE),
        vregs(SIDE),
        vregs(36),
        vregs(36),
        vregs(FULL),
        vregs(FULL),
        moduli_rows,
    )
    *arrays, edge, norms = call(
        early_kernel,
        (
            *shared,
            vregs(24),
            pltpu.VMEM((8, SPAN), F32),
        ),
    )(own)
    from_z = lax.ppermute(to_z, TILE, in_z)
    from_y = lax.ppermute(to_y, TILE, in_y)
    pairs_a, pairs_b, base_a, base_b, to_a, to_b, rows, probes_block = call(
        inner_kernel,
        (*shared, pltpu.VMEM((8, 2 * HALF * SPAN), F32)),
        aliases={3 + i: i for i in range(7)},
    )(from_y, from_z, edge, *arrays)
    half_block = pltpu.VMEM((8, HALF * SPAN), F32)
    from_b = lax.ppermute(to_b, LAYER, in_chip)
    from_a = lax.ppermute(to_a, LAYER, in_core)
    planes = lax.axis_size(PLANE)
    columns = lax.axis_size(COLUMN)
    scratch = (pltpu.VMEM((SIDE, 8, SPAN), F32), pltpu.VMEM((32, SPAN), F32))
    near_a, one_block_a, two_a = call(
        side_a_kernel,
        (vregs(SIDE), half_block, vregs(HALF)),
        scratch=(*scratch, pltpu.VMEM((SIDE, 8, SPAN), F32)),
    )(from_a, pairs_a, base_a, rows)
    block, message = call(
        side_b_kernel,
        (pltpu.VMEM((24, 2 * HALF * SPAN), F32), pltpu.VMEM((planes, 2, SPAN), F32)),
        scratch=(
            *scratch,
            pltpu.VMEM((SIDE, 8, SPAN), F32),
            pltpu.VMEM((SIDE, 8, SPAN), F32),
            half_block,
        ),
    )(from_b, pairs_b, base_b, rows, near_a, one_block_a, two_a, probes_block, norms)
    parts = lax.all_to_all(message, PLANE, 0, 0, tiled=True)
    message = call(total_kernel, pltpu.VMEM((columns, 2, SPAN), F32))(parts)
    parts = lax.all_to_all(message, COLUMN, 0, 0, tiled=True)
    rows = jax.ShapeDtypeStruct((PROBES * ROWS, SPAN), F32)
    solution_rows, residual_rows = call(final_kernel, (rows, rows))(parts, block)
    return solution_rows.reshape(probes.shape), residual_rows.reshape(probes.shape)


def solution(mesh):
    split = Mesh(
        mesh.devices.reshape(4, 16, 2, 2, 2), ("tile_0", "tile_1", "tile_2", "layer_0", "layer_1")
    )
    spread = P(None, None, LAYER, TILE, None)
    return jax.shard_map(
        body,
        mesh=split,
        in_specs=(spread, P(LAYER, TILE, None), P()),
        out_specs=(spread, spread),
        check_vma=False,
    )
```
